32 devices in a mesh: dp: 8 (over y, x, core), mp: 4 (over z).
Axes of the slice: x: 2, y: 2, z: 4, core: 2. Of those that a mesh axis runs over, the one named last changes fastest.
Arguments:
- pre: bfloat16 [1024, 12288], P('dp', 'mp'), may hold values from -32 to 32
- weight: float32 [6144, 12288], P('dp', 'mp'), may hold values from -0.0546875 to 0.0546875
- target: bfloat16 [6144, 1024], P('dp'), may hold values from -100 to 100
Outputs:
- update: float32 [6144, 12288], P('dp', 'mp')
The draws below stay inside these ranges and needn't reach their ends.
All inputs are finite; a program needn't handle non-finite values.
Results may differ from the reference program's by a relative error of at most 0.0003.
The reference program's roundings to bfloat16 on the way count: a program that leaves them out, or rounds other values in their place, can miss the bound.
Values may be sent and summed in bfloat16 or wider, within the bound.
A program may use at most 64 MiB of HBM per device.

```python
import jax
import jax.numpy as jnp

D = 6144
FF = 12288
TOKENS = 1024


def draw_pre(key, part):
    first, second = jax.random.split(key, 2)
    ramp = jnp.arange(FF, dtype=jnp.float32) / max(FF - 1, 1)
    spread = 10.0 ** jax.random.uniform(second, (FF,), jnp.float32)
    scale = 0.25 * 3.0 ** ramp * spread
    base = jax.random.truncated_normal(first, -4.0, 4.0, (TOKENS, FF), jnp.float32)
    values = scale * base
    return values.astype(jnp.bfloat16)


def draw_target(key, part):
    first, second = jax.random.split(key, 2)
    ramp = jnp.arange(D, dtype=jnp.float32) / max(D - 1, 1)
    spread = 10.0 ** jax.random.uniform(second, (D,), jnp.float32)
    scale = 0.5 * 3.0 ** ramp * spread
    base = jax.random.truncated_normal(first, -4.0, 4.0, (D, TOKENS), jnp.float32)
    values = scale[:, None] * base
    return values.astype(jnp.bfloat16)


def block_levels(own_key, dims, shards, least, top_value):
    def one(axis_at, blocks):
        steps = jax.random.uniform(jax.random.fold_in(jax.random.fold_in(own_key, 6), axis_at), (blocks,), jnp.float32, least / len(shards), top_value / len(shards))
        return jnp.repeat(jnp.exp(steps), dims[axis_at] // blocks).reshape((-1,) + (1,) * (len(dims) - axis_at - 1))

    gain = one(*shards[0])
    for cut in shards[1:]:
        gain = gain * one(*cut)
    return gain


def normal_values(rng, shape, scale, limit, shards=(), kind=jnp.bfloat16):
    drawn = scale * jax.random.normal(rng, shape, jnp.float32)
    if shards:
        drawn = drawn * block_levels(rng, shape, shards, -0.22, 0.18)
    return jnp.clip(drawn, -limit, limit).astype(kind)


def setup_inputs(seed: int = 0) -> dict:
    seeds = jax.random.split(jax.random.key(seed), 4)
    return {
        "pre": draw_pre(jax.random.fold_in(seeds[3], 71), 0),
        "weight": normal_values(seeds[1], (D, FF), FF ** -0.5, 0.0546875, ((0, 8), (1, 4)), jnp.float32),
        "target": draw_target(jax.random.fold_in(seeds[3], 71), 0),
    }


radius = 0.005
epsilon = 1e-06

def residual_of(matrix, hidden, target):
    out = jnp.dot(matrix, hidden.T, preferred_element_type=jnp.float32)
    return (out - target.astype(jnp.float32)).astype(jnp.bfloat16)

def reference(pre, weight, target):
    hidden = jax.nn.gelu(pre.astype(jnp.float32), approximate=False).astype(jnp.bfloat16)
    resid = residual_of(weight.astype(jnp.bfloat16), hidden, target)
    ascent = jnp.dot(resid, hidden, preferred_element_type=jnp.float32)
    ascent_ms = jnp.mean(ascent * ascent)
    perturbed = (weight + radius * jnp.tanh(ascent / jnp.sqrt(ascent_ms + epsilon))).astype(jnp.bfloat16)
    resid_two = residual_of(perturbed, hidden, target)
    descent = jnp.dot(resid_two, hidden, preferred_element_type=jnp.float32)
    descent_ms = jnp.mean(descent * descent)
    return descent / jnp.sqrt(descent_ms + epsilon)
```

```python
import functools

import jax
import jax.numpy as jnp
from jax import lax
from jax.experimental import pallas as pl
from jax.experimental.pallas import tpu as pltpu
from jax.sharding import PartitionSpec as P

radius = 0.005
epsilon = 1e-06
MESH = pl.DeviceIdType.MESH
f32, bf16 = jnp.float32, jnp.bfloat16
TILE = 256


def on_device_plain(pre, weight, target):
    hidden = jax.nn.gelu(pre.astype(jnp.float32), approximate=False).astype(jnp.bfloat16)
    everyone = lax.all_gather(hidden, "dp", axis=0, tiled=True)
    entries = weight.shape[0] * weight.shape[1] * lax.axis_size("dp") * lax.axis_size("mp")

    def residual_of(matrix):
        partial_out = lax.dot_general(
            matrix, everyone, (((1,), (1,)), ((), ())), preferred_element_type=jnp.float32
        )
        summed = lax.psum(partial_out, "mp")
        return (summed - target.astype(jnp.float32)).astype(jnp.bfloat16)

    resid = residual_of(weight.astype(jnp.bfloat16))
    ascent = jnp.dot(resid, everyone, preferred_element_type=jnp.float32)
    ascent_ms = lax.psum(jnp.sum(ascent * ascent), ("dp", "mp")) / entries
    perturbed = (weight + radius * jnp.tanh(ascent / jnp.sqrt(ascent_ms + epsilon))).astype(
        jnp.bfloat16
    )
    resid_two = residual_of(perturbed)
    descent = jnp.dot(resid_two, everyone, preferred_element_type=jnp.float32)
    descent_ms = lax.psum(jnp.sum(descent * descent), ("dp", "mp")) / entries
    return descent / jnp.sqrt(descent_ms + epsilon)


NEAR = (
    2.326819970068386e-2, -1.387039388740657e-1, 3.687424674597105e-1, -5.824733027278666e-1,
    6.210004621745983e-1, -4.944515323274145e-1, 3.404879937665872e-1, -2.741127028184656e-1,
    5.638259427386472e-1,
)
FAR = (
    -1.047766399936249e1, 1.297719955372516e1, -7.495518717768503e0, 2.921019019210786e0,
    -1.015265279202700e0, 4.218463358204948e-1, -2.820767439740514e-1, 5.641895067754075e-1,
)


def poly(coefficients, y):
    out = jnp.full_like(y, coefficients[0])
    for k in coefficients[1:]:
        out = out * y + k
    return out


def gelu(x):
    s = x * 0.7071067811865476
    t = jnp.maximum(-s, 1.0)
    q = 1.0 / t
    y = q * q
    tail = jnp.exp(-t * t) * q * jnp.where(t < 2.0, poly(NEAR, y), poly(FAR, y))
    return 0.5 * x * jnp.where(s > -1.0, 1.0 + lax.erf(s), tail)


def encode(x):
    return (x * jnp.abs(x)).astype(bf16)


def decode(y):
    y = y.astype(f32)
    return y * lax.rsqrt(jnp.maximum(jnp.abs(y), 1e-37))


def kernel(
    N, M, entries,
    pre_hbm, w_hbm, t_hbm, a, tot_ref,
    w, wl, h, x, tg, own, up_out, dn_out, up_in, dn_in, ssq, sm, sd,
    ld, ags, agr, cs, cr, ss, sr,
):
    rows, ff = w.shape
    tokens = tg.shape[1]
    blk = tokens // N
    R = rows // TILE
    G = tokens // TILE
    C = R * G
    dp = lax.axis_index("dp")
    z = lax.axis_index("mp")
    b0 = lax.rem(dp, 2)
    b1 = lax.rem(dp // 2, 2)
    b2 = dp // 4
    ds_ = 1 - 2 * b0
    dx = 2 * (1 - 2 * b1)
    dy = 4 * (1 - 2 * b2)
    sib = dp + ds_
    p = dp + (1 - b0) * dx + b0 * dy
    q = dp + b0 * dx + (1 - b0) * dy
    diag = dp + dx + dy
    sibp = q + ds_
    sibq = p + ds_
    sibd = diag + ds_

    def load(i, src, dst):
        return pltpu.make_async_copy(src, dst, ld.at[i])

    def tok(b, lo=0, n=blk):
        return pl.ds(pl.multiple_of(b * blk + lo, 16), n)

    def rowg(r):
        return pl.ds(pl.multiple_of(r * TILE, TILE), TILE)

    load_x = load(0, pre_hbm, x)
    load_t = load(1, t_hbm, tg)
    load_w = [load(2 + r, w_hbm.at[rowg(r), :], w.at[rowg(r), :]) for r in range(R)]
    load_x.start()
    for lw in load_w:
        lw.start()
    load_t.start()

    barrier = pltpu.get_barrier_semaphore()
    for k in range(1, N):
        pl.semaphore_signal(barrier, inc=1, device_id=(lax.rem(dp + k, N), z), device_id_type=MESH)
    for k in range(1, M):
        pl.semaphore_signal(barrier, inc=1, device_id=(dp, lax.rem(z + k, M)), device_id_type=MESH)

    load_x.wait()

    def activate(i, _):
        rs = pl.ds(pl.multiple_of(i * 16, 16), 16)
        h[tok(dp, i * 16, 16), :] = gelu(x[rs, :].astype(f32)).astype(bf16)
        return 0

    lax.fori_loop(0, blk // 16, activate, 0)
    pl.semaphore_wait(barrier, N + M - 2)

    def gather(i, block, to, lo=0, n=blk):
        return pltpu.make_async_remote_copy(
            src_ref=h.at[tok(block, lo, n), :], dst_ref=h.at[tok(block, lo, n), :],
            send_sem=ags.at[i], recv_sem=agr.at[i],
            device_id=(to, z), device_id_type=MESH,
        )

    hb = blk // 2
    S, PP, Q, SP, SQ, RPQ, RQP, SD = range(8)
    sends = {
        S: gather(S, dp, sib), PP: gather(PP, dp, p), Q: gather(Q, dp, q),
        SP: gather(SP, p, sib), SQ: gather(SQ, q, sib),
        RPQ: gather(RPQ, p, q, 0, hb), RQP: gather(RQP, q, p, hb, hb),
        SD: gather(SD, diag, sib),
    }
    recvs = {
        S: gather(S, sib, sib), PP: gather(PP, p, p), Q: gather(Q, q, q),
        SP: gather(SP, sibp, sib), SQ: gather(SQ, sibq, sib),
        RPQ: gather(RPQ, diag, q, 0, hb), RQP: gather(RQP, diag, p, hb, hb),
        SD: gather(SD, sibd, sib),
    }
    sends[PP].start()
    sends[S].start()

    def cast(r):
        def run(i, _):
            rs = pl.ds(pl.multiple_of(r * TILE + i * 64, 64), 64)
            wl[rs, :] = w[rs, :].astype(bf16)
            return 0

        load_w[r].wait()
        lax.fori_loop(0, TILE // 64, run, 0)

    for r in range(R):
        cast(r)
    load_t.wait()

    @pl.when(z == 0)
    def _():
        up_in[...] = jnp.zeros_like(up_in)

    @pl.when(z == M - 1)
    def _():
        dn_in[...] = jnp.zeros_like(dn_in)

    order = [dp, sib, p, sibp, q, sibq, diag, sibd]

    def block_of(c):
        out = order[0] * 0
        for k in range(N):
            out = out + order[k] * (1 - jnp.minimum(jnp.abs(c - k), 1))
        return out

    UP, DOWN = range(2)
    zu = lax.rem(z + 1, M)
    zd = lax.rem(z + M - 1, M)

    def up(c):
        return pltpu.make_async_remote_copy(
            src_ref=up_out.at[c], dst_ref=up_in.at[c], send_sem=cs.at[UP, c], recv_sem=cr.at[UP, c],
            device_id=(dp, zu), device_id_type=MESH,
        )

    def down(c):
        return pltpu.make_async_remote_copy(
            src_ref=dn_out.at[c], dst_ref=dn_in.at[c], send_sem=cs.at[DOWN, c], recv_sem=cr.at[DOWN, c],
            device_id=(dp, zd), device_id_type=MESH,
        )

    def chain(produce, consume):
        lag_up = 2 * z
        lag_dn = 2 * (M - 1 - z)
        lag = jnp.maximum(lag_up, lag_dn)

        def inside(c):
            return (c >= 0) & (c < C)

        def step(s, _):
            @pl.when(s < C)
            def _():
                produce(s)

                @pl.when(z == 0)
                def _():
                    up_out[s] = encode(own[s])
                    up(s).start()

                @pl.when(z == M - 1)
                def _():
                    dn_out[s] = encode(own[s])
                    down(s).start()

            cu = s - lag_up

            @pl.when((z > 0) & inside(cu))
            def _():
                up(cu).wait_recv()

                @pl.when(z < M - 1)
                def _():
                    up_out[cu] = encode(own[cu] + decode(up_in[cu]))
                    up(cu).start()

            cd = s - lag_dn

            @pl.when((z < M - 1) & inside(cd))
            def _():
                down(cd).wait_recv()

                @pl.when(z > 0)
                def _():
                    dn_out[cd] = encode(own[cd] + decode(dn_in[cd]))
                    down(cd).start()

            c = s - lag

            @pl.when(inside(c))
            def _():
                consume(c)

            return 0

        lax.fori_loop(0, C + 2 * (M - 1), step, 0)

        def drain(c, _):
            @pl.when(z < M - 1)
            def _():
                up(c).wait_send()

            @pl.when(z > 0)
            def _():
                down(c).wait_send()

            return 0

        lax.fori_loop(0, C, drain, 0)

    def summed(c):
        return own[c] + decode(up_in[c]) + decode(dn_in[c])

    def squares(d):
        return (d * d).reshape(d.shape[0] // 8, 8, d.shape[1]).sum(axis=0)

    def gradient(resid, rs, g, right):
        d = jnp.dot(resid, right, preferred_element_type=f32)

        @pl.when(g == 0)
        def _():
            a[rs, :] = d

        @pl.when((g > 0) & (g < G - 1))
        def _():
            a[rs, :] += d

        @pl.when(g == G - 1)
        def _():
            total = a[rs, :] + d
            a[rs, :] = total
            ssq[...] += squares(total)

    def pair(g):
        return block_of(2 * g), block_of(2 * g + 1)

    def hidden_of(g):
        one, two = pair(g)
        return jnp.concatenate([h[tok(one), :], h[tok(two), :]], axis=0)

    def produce_one(s):
        g = s // R
        r = lax.rem(s, R)

        @pl.when(s == 0)
        def _():
            recvs[S].wait_recv()

        @pl.when(s == R)
        def _():
            recvs[PP].wait_recv()
            sends[SP].start()
            sends[Q].start()
            recvs[SP].wait_recv()

        @pl.when(s == 2 * R)
        def _():
            recvs[Q].wait_recv()
            sends[RPQ].start()
            sends[RQP].start()
            sends[SQ].start()
            recvs[SQ].wait_recv()

        @pl.when(s == 3 * R)
        def _():
            recvs[RPQ].wait_recv()
            recvs[RQP].wait_recv()
            sends[SD].start()
            recvs[SD].wait_recv()

        own[s] = lax.dot_general(
            wl[rowg(r), :], hidden_of(g), (((1,), (1,)), ((), ())), preferred_element_type=f32
        )

    def consume_one(c):
        g = c // R
        rs = rowg(lax.rem(c, R))
        one, two = pair(g)
        target = jnp.concatenate(
            [tg[rs, pl.ds(pl.multiple_of(b * blk, blk), blk)] for b in (one, two)], axis=1
        )
        resid = (summed(c) - target.astype(f32)).astype(bf16)
        gradient(resid, rs, g, hidden_of(g))

    ssq[...] = jnp.zeros_like(ssq)
    chain(produce_one, consume_one)
    for i in range(8):
        sends[i].wait_send()

    def total_squares(rnd):
        v = ssq[...]
        part = v[:, 0:128]
        for k in range(1, v.shape[1] // 128):
            part = part + v[:, 128 * k:128 * (k + 1)]

        def small(buf, lane, i, me, to):
            return pltpu.make_async_remote_copy(
                src_ref=buf.at[me], dst_ref=buf.at[me],
                send_sem=ss.at[rnd, lane, i], recv_sem=sr.at[rnd, lane, i],
                device_id=to, device_id_type=MESH,
            )

        mb = sm.at[rnd]
        db = sd.at[rnd]
        mb[z] = part
        upz = [(dp, lax.rem(z + k, M)) for k in range(M)]
        dnz = [lax.rem(z + M - k, M) for k in range(M)]
        for k in range(1, M):
            small(mb, 0, k, z, upz[k]).start()
        for k in range(1, M):
            small(mb, 0, k, dnz[k], upz[k]).wait_recv()
        for k in range(1, M):
            small(mb, 0, k, z, upz[k]).wait_send()
        got = mb[0]
        for k in range(1, M):
            got = got + mb[k]
        db[dp] = got
        upd = [(lax.rem(dp + k, N), z) for k in range(N)]
        dnd = [lax.rem(dp + N - k, N) for k in range(N)]
        for k in range(1, N):
            small(db, 1, k, dp, upd[k]).start()
        for k in range(1, N):
            small(db, 1, k, dnd[k], upd[k]).wait_recv()
        for k in range(1, N):
            small(db, 1, k, dp, upd[k]).wait_send()
        got = db[0]
        for k in range(1, N):
            got = got + db[k]
        return jnp.sum(jnp.sum(got, axis=0, keepdims=True), axis=1, keepdims=True)

    scale = 1.0 / jnp.sqrt(total_squares(0) / entries + epsilon)
    ssq[...] = jnp.zeros_like(ssq)

    def wide_cols(g):
        return pl.ds(pl.multiple_of(g * TILE, TILE), TILE)

    def produce_two(s):
        r = s // G
        g = lax.rem(s, G)

        @pl.when(g == 0)
        def _():
            def perturb(i, _):
                rs = pl.ds(pl.multiple_of(r * TILE + i * 16, 16), 16)
                wl[rs, :] = (w[rs, :] + radius * jnp.tanh(a[rs, :] * scale)).astype(bf16)
                return 0

            lax.fori_loop(0, TILE // 16, perturb, 0)

        own[s] = lax.dot_general(
            wl[rowg(r), :], h[wide_cols(g), :], (((1,), (1,)), ((), ())), preferred_element_type=f32
        )

    def consume_two(c):
        g = lax.rem(c, G)
        rs = rowg(c // G)
        resid = (summed(c) - tg[rs, wide_cols(g)].astype(f32)).astype(bf16)
        gradient(resid, rs, g, h[wide_cols(g), :])

    chain(produce_two, consume_two)
    tot_ref[...] = 1.0 / jnp.sqrt(total_squares(1) / entries + epsilon)


def on_device(N, M, pre, weight, target):
    rows, ff = weight.shape
    tokens = target.shape[1]
    entries = rows * ff * N * M
    C = (rows // TILE) * (tokens // TILE)
    any_ = pl.BlockSpec(memory_space=pl.ANY)
    descent, scale = pl.pallas_call(
        functools.partial(kernel, N, M, float(entries)),
        out_shape=(pltpu.VMEM((rows, ff), f32), pltpu.VMEM((1, 1), f32)),
        in_specs=[any_, any_, any_],
        scratch_shapes=[
            pltpu.VMEM((rows, ff), f32),
            pltpu.VMEM((rows, ff), bf16),
            pltpu.VMEM((tokens, ff), bf16),
            pltpu.VMEM((tokens // N, ff), bf16),
            pltpu.VMEM((rows, tokens), bf16),
            pltpu.VMEM((C, TILE, TILE), f32),
            pltpu.VMEM((C, TILE, TILE), bf16),
            pltpu.VMEM((C, TILE, TILE), bf16),
            pltpu.VMEM((C, TILE, TILE), bf16),
            pltpu.VMEM((C, TILE, TILE), bf16),
            pltpu.VMEM((8, ff), f32),
            pltpu.VMEM((2, M, 8, 128), f32),
            pltpu.VMEM((2, N, 8, 128), f32),
            pltpu.SemaphoreType.DMA((2 + rows // TILE,)),
            pltpu.SemaphoreType.DMA((8,)),
            pltpu.SemaphoreType.DMA((8,)),
            pltpu.SemaphoreType.DMA((2, C)),
            pltpu.SemaphoreType.DMA((2, C)),
            pltpu.SemaphoreType.DMA((2, 2, max(N, M))),
            pltpu.SemaphoreType.DMA((2, 2, max(N, M))),
        ],
        compiler_params=pltpu.CompilerParams(
            collective_id=0, has_side_effects=True, vmem_limit_bytes=44 << 20
        ),
    )(pre, weight, target)
    return descent * scale[0, 0]


def solution(mesh):
    N, M = mesh.shape["dp"], mesh.shape["mp"]
    body = functools.partial(on_device, N, M) if (N, M) == (8, 4) else on_device_plain
    return jax.shard_map(
        body,
        mesh=mesh,
        in_specs=(P("dp", "mp"), P("dp", "mp"), P("dp", None)),
        out_specs=P("dp", "mp"),
        check_vma=False,
    )
```

```python
import functools

import jax
import jax.numpy as jnp
from jax import lax
from jax.experimental import pallas as pl
from jax.experimental.pallas import tpu as pltpu
from jax.sharding import PartitionSpec as P

radius = 0.005
epsilon = 1e-06
MESH = pl.DeviceIdType.MESH
f32, bf16 = jnp.float32, jnp.bfloat16
TILE = 256
PIECES = 2
LAGS = (3, 3)


def on_device_plain(pre, weight, target):
    hidden = jax.nn.gelu(pre.astype(jnp.float32), approximate=False).astype(jnp.bfloat16)
    everyone = lax.all_gather(hidden, "dp", axis=0, tiled=True)
    entries = weight.shape[0] * weight.shape[1] * lax.axis_size("dp") * lax.axis_size("mp")

    def residual_of(matrix):
        partial_out = lax.dot_general(
            matrix, everyone, (((1,), (1,)), ((), ())), preferred_element_type=jnp.float32
        )
        summed = lax.psum(partial_out, "mp")
        return (summed - target.astype(jnp.float32)).astype(jnp.bfloat16)

    resid = residual_of(weight.astype(jnp.bfloat16))
    ascent = jnp.dot(resid, everyone, preferred_element_type=jnp.float32)
    ascent_ms = lax.psum(jnp.sum(ascent * ascent), ("dp", "mp")) / entries
    perturbed = (weight + radius * jnp.tanh(ascent / jnp.sqrt(ascent_ms + epsilon))).astype(
        jnp.bfloat16
    )
    resid_two = residual_of(perturbed)
    descent = jnp.dot(resid_two, everyone, preferred_element_type=jnp.float32)
    descent_ms = lax.psum(jnp.sum(descent * descent), ("dp", "mp")) / entries
    return descent / jnp.sqrt(descent_ms + epsilon)


NEAR = (
    2.326819970068386e-2, -1.387039388740657e-1, 3.687424674597105e-1, -5.824733027278666e-1,
    6.210004621745983e-1, -4.944515323274145e-1, 3.404879937665872e-1, -2.741127028184656e-1,
    5.638259427386472e-1,
)
FAR = (
    -1.047766399936249e1, 1.297719955372516e1, -7.495518717768503e0, 2.921019019210786e0,
    -1.015265279202700e0, 4.218463358204948e-1, -2.820767439740514e-1, 5.641895067754075e-1,
)


def poly(coefficients, y):
    out = jnp.full_like(y, coefficients[0])
    for k in coefficients[1:]:
        out = out * y + k
    return out


def gelu(x):
    s = x * 0.7071067811865476
    t = jnp.maximum(-s, 1.0)
    q = 1.0 / t
    y = q * q
    tail = jnp.exp(-t * t) * q * jnp.where(t < 2.0, poly(NEAR, y), poly(FAR, y))
    return 0.5 * x * jnp.where(s > -1.0, 1.0 + lax.erf(s), tail)


def encode(x):
    return (x * jnp.abs(x)).astype(bf16)


def decode(y):
    y = y.astype(f32)
    return y * lax.rsqrt(jnp.maximum(jnp.abs(y), 1e-37))


def kernel(
    N, M, entries,
    pre_hbm, w_hbm, t_hbm, a, tot_ref,
    w, wl, h, x, tg, own, up_out, dn_out, up_in, dn_in, ssq, sm,
    ld, ags, agr, cs, cr, ss, sr,
):
    rows, ff = w.shape
    tokens = tg.shape[1]
    blk = tokens // N
    R = rows // TILE
    G = tokens // TILE
    C = R * G
    dp = lax.axis_index("dp")
    z = lax.axis_index("mp")
    b0 = lax.rem(dp, 2)
    b1 = lax.rem(dp // 2, 2)
    b2 = dp // 4
    ds_ = 1 - 2 * b0
    dx = 2 * (1 - 2 * b1)
    dy = 4 * (1 - 2 * b2)
    sib = dp + ds_
    p = dp + (1 - b0) * dx + b0 * dy
    q = dp + b0 * dx + (1 - b0) * dy
    diag = dp + dx + dy
    sibp = q + ds_
    sibq = p + ds_
    sibd = diag + ds_

    def load(i, src, dst):
        return pltpu.make_async_copy(src, dst, ld.at[i])

    def tok(b, lo=0, n=blk):
        return pl.ds(pl.multiple_of(b * blk + lo, 16), n)

    def rowg(r):
        return pl.ds(pl.multiple_of(r * TILE, TILE), TILE)

    load_x = load(0, pre_hbm, x)
    load_t = load(1, t_hbm, tg)
    load_w = [load(2 + r, w_hbm.at[rowg(r), :], w.at[rowg(r), :]) for r in range(R)]
    load_x.start()
    for lw in load_w:
        lw.start()
    load_t.start()

    barrier = pltpu.get_barrier_semaphore()
    me = dp * M + z

    def peer(k):
        other = lax.rem(me + k, N * M)
        return other // M, lax.rem(other, M)

    def greet(k, _):
        pl.semaphore_signal(barrier, inc=1, device_id=peer(k), device_id_type=MESH)
        return 0

    lax.fori_loop(1, N * M, greet, 0)

    load_x.wait()

    def activate(i, _):
        rs = pl.ds(pl.multiple_of(i * 16, 16), 16)
        h[tok(dp, i * 16, 16), :] = gelu(x[rs, :].astype(f32)).astype(bf16)
        return 0

    lax.fori_loop(0, blk // 16, activate, 0)
    pl.semaphore_wait(barrier, N * M - 1)

    def gather(i, block, to):
        return pltpu.make_async_remote_copy(
            src_ref=h.at[tok(block), :], dst_ref=h.at[tok(block), :],
            send_sem=ags.at[i], recv_sem=agr.at[i],
            device_id=(to, z), device_id_type=MESH,
        )

    S, PP, SP, T, ST, RL, SR = range(7)
    sends = {
        S: gather(S, dp, sib), PP: gather(PP, dp, p), SP: gather(SP, p, sib), T: gather(T, sib, p),
        ST: gather(ST, sibq, sib), RL: gather(RL, sibp, p), SR: gather(SR, sibd, sib),
    }
    recvs = {
        S: gather(S, sib, sib), PP: gather(PP, p, p), SP: gather(SP, sibp, sib), T: gather(T, sibq, p),
        ST: gather(ST, q, sib), RL: gather(RL, sibd, p), SR: gather(SR, diag, sib),
    }
    sends[PP].start()
    sends[S].start()

    def cast(r):
        def run(i, _):
            rs = pl.ds(pl.multiple_of(r * TILE + i * 64, 64), 64)
            wl[rs, :] = w[rs, :].astype(bf16)
            return 0

        load_w[r].wait()
        lax.fori_loop(0, TILE // 64, run, 0)

    load_t.wait()

    @pl.when(z == 0)
    def _():
        up_in[...] = jnp.zeros_like(up_in)

    @pl.when(z == M - 1)
    def _():
        dn_in[...] = jnp.zeros_like(dn_in)

    order = [dp, sib, p, sibp, sibq, q, sibd, diag]

    def block_of(c):
        out = order[0] * 0
        for k in range(N):
            out = out + order[k] * (1 - jnp.minimum(jnp.abs(c - k), 1))
        return out

    UP, DOWN = range(2)
    zu = lax.rem(z + 1, M)
    zd = lax.rem(z + M - 1, M)

    def up(c):
        return pltpu.make_async_remote_copy(
            src_ref=up_out.at[c], dst_ref=up_in.at[c], send_sem=cs.at[UP, c], recv_sem=cr.at[UP, c],
            device_id=(dp, zu), device_id_type=MESH,
        )

    def down(c):
        return pltpu.make_async_remote_copy(
            src_ref=dn_out.at[c], dst_ref=dn_in.at[c], send_sem=cs.at[DOWN, c], recv_sem=cr.at[DOWN, c],
            device_id=(dp, zd), device_id_type=MESH,
        )

    K = up_out.shape[0] // C
    sub = TILE // K

    def store_own(t, d):
        for k in range(K):
            own[t * K + k] = d[k * sub:(k + 1) * sub]

    def chain(hop, produce, consume):
        lag_up = hop * z
        lag_dn = hop * (M - 1 - z)
        lag = jnp.maximum(lag_up, lag_dn)

        def inside(c):
            return (c >= 0) & (c < C * K)

        def step(s, _):
            cu = s - lag_up

            @pl.when((z > 0) & inside(cu))
            def _():
                up(cu).wait_recv()

                @pl.when(z < M - 1)
                def _():
                    up_out[cu] = encode(own[cu] + decode(up_in[cu]))
                    up(cu).start()

            cd = s - lag_dn

            @pl.when((z < M - 1) & inside(cd))
            def _():
                down(cd).wait_recv()

                @pl.when(z > 0)
                def _():
                    dn_out[cd] = encode(own[cd] + decode(dn_in[cd]))
                    down(cd).start()

            @pl.when((s < C * K) & (lax.rem(s, K) == 0))
            def _():
                produce(s // K)

                @pl.when(z == 0)
                def _():
                    for k in range(K):
                        up_out[s + k] = encode(own[s + k])
                        up(s + k).start()

                @pl.when(z == M - 1)
                def _():
                    for k in range(K):
                        dn_out[s + k] = encode(own[s + k])
                        down(s + k).start()

            c = s - lag

            @pl.when(inside(c) & (lax.rem(c, K) == K - 1))
            def _():
                consume(c // K)

            return 0

        lax.fori_loop(0, C * K + hop * (M - 1), step, 0)

        def drain(c, _):
            @pl.when(z < M - 1)
            def _():
                up(c).wait_send()

            @pl.when(z > 0)
            def _():
                down(c).wait_send()

            return 0

        lax.fori_loop(0, C * K, drain, 0)

    def summed(t):
        return jnp.concatenate(
            [own[t * K + k] + decode(up_in[t * K + k]) + decode(dn_in[t * K + k]) for k in range(K)], axis=0
        )

    def squares(d):
        return (d * d).reshape(d.shape[0] // 8, 8, d.shape[1]).sum(axis=0)

    def gradient(resid, rs, g, right):
        d = jnp.dot(resid, right, preferred_element_type=f32)

        @pl.when(g == 0)
        def _():
            a[rs, :] = d

        @pl.when((g > 0) & (g < G - 1))
        def _():
            a[rs, :] += d

        @pl.when(g == G - 1)
        def _():
            total = a[rs, :] + d
            a[rs, :] = total
            ssq[...] += squares(total)

    def pair(g):
        return block_of(2 * g), block_of(2 * g + 1)

    def hidden_of(g):
        one, two = pair(g)
        return jnp.concatenate([h[tok(one), :], h[tok(two), :]], axis=0)

    def produce_one(s):
        g = s // R
        r = lax.rem(s, R)

        for k in range(R):
            @pl.when(s == k)
            def _():
                cast(k)

        @pl.when(s == 0)
        def _():
            recvs[S].wait_recv()
            sends[T].start()

        @pl.when(s == R)
        def _():
            recvs[PP].wait_recv()
            sends[SP].start()
            recvs[SP].wait_recv()
            sends[RL].start()

        @pl.when(s == 2 * R)
        def _():
            recvs[T].wait_recv()
            sends[ST].start()
            recvs[ST].wait_recv()

        @pl.when(s == 3 * R)
        def _():
            recvs[RL].wait_recv()
            sends[SR].start()
            recvs[SR].wait_recv()

        store_own(s, lax.dot_general(
            wl[rowg(r), :], hidden_of(g), (((1,), (1,)), ((), ())), preferred_element_type=f32
        ))

    def consume_one(c):
        g = c // R
        rs = rowg(lax.rem(c, R))
        one, two = pair(g)
        target = jnp.concatenate(
            [tg[rs, pl.ds(pl.multiple_of(b * blk, blk), blk)] for b in (one, two)], axis=1
        )
        resid = (summed(c) - target.astype(f32)).astype(bf16)
        gradient(resid, rs, g, hidden_of(g))

    ssq[...] = jnp.zeros_like(ssq)
    chain(LAGS[0], produce_one, consume_one)
    for i in range(7):
        sends[i].wait_send()

    def total_squares(rnd):
        v = ssq[...]
        part = v[:, 0:128]
        for k in range(1, v.shape[1] // 128):
            part = part + v[:, 128 * k:128 * (k + 1)]

        def small(k, src, to):
            return pltpu.make_async_remote_copy(
                src_ref=sm.at[rnd, src], dst_ref=sm.at[rnd, src],
                send_sem=ss.at[rnd, k], recv_sem=sr.at[rnd, k],
                device_id=to, device_id_type=MESH,
            )

        sm[rnd, me] = part.sum(axis=0, keepdims=True)

        def start(k, _):
            small(k, me, peer(k)).start()
            return 0

        def arrive(k, _):
            small(k, lax.rem(me + N * M - k, N * M), peer(k)).wait_recv()
            return 0

        def leave(k, _):
            small(k, me, peer(k)).wait_send()
            return 0

        lax.fori_loop(1, N * M, start, 0)
        lax.fori_loop(1, N * M, arrive, 0)
        lax.fori_loop(1, N * M, leave, 0)
        got = sm[rnd].sum(axis=0)
        return jnp.sum(got, axis=1, keepdims=True)

    scale = 1.0 / jnp.sqrt(total_squares(0) / entries + epsilon)
    ssq[...] = jnp.zeros_like(ssq)

    def wide_cols(g):
        return pl.ds(pl.multiple_of(g * TILE, TILE), TILE)

    def produce_two(s):
        r = s // G
        g = lax.rem(s, G)

        @pl.when(g == 0)
        def _():
            def perturb(i, _):
                rs = pl.ds(pl.multiple_of(r * TILE + i * 16, 16), 16)
                wl[rs, :] = (w[rs, :] + radius * jnp.tanh(a[rs, :] * scale)).astype(bf16)
                return 0

            lax.fori_loop(0, TILE // 16, perturb, 0)

        store_own(s, lax.dot_general(
            wl[rowg(r), :], h[wide_cols(g), :], (((1,), (1,)), ((), ())), preferred_element_type=f32
        ))

    def consume_two(c):
        g = lax.rem(c, G)
        rs = rowg(c // G)
        resid = (summed(c) - tg[rs, wide_cols(g)].astype(f32)).astype(bf16)
        gradient(resid, rs, g, h[wide_cols(g), :])

    chain(LAGS[1], produce_two, consume_two)
    tot_ref[...] = 1.0 / jnp.sqrt(total_squares(1) / entries + epsilon)


def finish(d_ref, s_ref, out_hbm, buf, sem):
    strips, n, _ = buf.shape

    def copy(i):
        return pltpu.make_async_copy(buf.at[i], out_hbm.at[pl.ds(i * n, n), :], sem.at[i])

    for i in range(strips):
        buf[i] = d_ref[i * n:(i + 1) * n, :] * s_ref[...]
        copy(i).start()
    for i in range(strips):
        copy(i).wait()


def on_device(N, M, pre, weight, target):
    rows, ff = weight.shape
    tokens = target.shape[1]
    entries = rows * ff * N * M
    C = (rows // TILE) * (tokens // TILE)
    sub = TILE // PIECES
    hbm = pl.BlockSpec(memory_space=pltpu.HBM)
    vmem = pl.BlockSpec(memory_space=pltpu.VMEM)
    descent, scale = pl.pallas_call(
        functools.partial(kernel, N, M, float(entries)),
        out_shape=(pltpu.VMEM((rows, ff), f32), pltpu.VMEM((1, 1), f32)),
        in_specs=[hbm, hbm, hbm],
        scratch_shapes=[
            pltpu.VMEM((rows, ff), f32),
            pltpu.VMEM((rows, ff), bf16),
            pltpu.VMEM((tokens, ff), bf16),
            pltpu.VMEM((tokens // N, ff), bf16),
            pltpu.VMEM((rows, tokens), bf16),
            pltpu.VMEM((C * PIECES, sub, TILE), f32),
            pltpu.VMEM((C * PIECES, sub, TILE), bf16),
            pltpu.VMEM((C * PIECES, sub, TILE), bf16),
            pltpu.VMEM((C * PIECES, sub, TILE), bf16),
            pltpu.VMEM((C * PIECES, sub, TILE), bf16),
            pltpu.VMEM((8, ff), f32),
            pltpu.VMEM((2, N * M, 1, 128), f32),
            pltpu.SemaphoreType.DMA((2 + rows // TILE,)),
            pltpu.SemaphoreType.DMA((7,)),
            pltpu.SemaphoreType.DMA((7,)),
            pltpu.SemaphoreType.DMA((2, C * PIECES)),
            pltpu.SemaphoreType.DMA((2, C * PIECES)),
            pltpu.SemaphoreType.DMA((2, N * M)),
            pltpu.SemaphoreType.DMA((2, N * M)),
        ],
        compiler_params=pltpu.CompilerParams(
            collective_id=0, has_side_effects=True, vmem_limit_bytes=44 << 20
        ),
    )(pre, weight, target)
    strips = 6
    return pl.pallas_call(
        finish,
        out_shape=jax.ShapeDtypeStruct((rows, ff), f32),
        in_specs=[vmem, vmem],
        out_specs=hbm,
        scratch_shapes=[
            pltpu.VMEM((strips, rows // strips, ff), f32),
            pltpu.SemaphoreType.DMA((strips,)),
        ],
        compiler_params=pltpu.CompilerParams(vmem_limit_bytes=24 << 20),
    )(descent, scale)


def solution(mesh):
    N, M = mesh.shape["dp"], mesh.shape["mp"]
    body = functools.partial(on_device, N, M) if (N, M) == (8, 4) else on_device_plain
    return jax.shard_map(
        body,
        mesh=mesh,
        in_specs=(P("dp", "mp"), P("dp", "mp"), P("dp", None)),
        out_specs=P("dp", "mp"),
        check_vma=False,
    )
```

```python
import functools

import jax
import jax.numpy as jnp
from jax import lax
from jax.experimental import pallas as pl
from jax.experimental.pallas import tpu as pltpu
from jax.sharding import PartitionSpec as P

radius = 0.005
epsilon = 1e-06
MESH = pl.DeviceIdType.MESH
f32, bf16 = jnp.float32, jnp.bfloat16
TILE = 256
PIECES = 2
LAGS = (3, 3)


def on_device_plain(pre, weight, target):
    hidden = jax.nn.gelu(pre.astype(jnp.float32), approximate=False).astype(jnp.bfloat16)
    everyone = lax.all_gather(hidden, "dp", axis=0, tiled=True)
    entries = weight.shape[0] * weight.shape[1] * lax.axis_size("dp") * lax.axis_size("mp")

    def residual_of(matrix):
        partial_out = lax.dot_general(
            matrix, everyone, (((1,), (1,)), ((), ())), preferred_element_type=jnp.float32
        )
        summed = lax.psum(partial_out, "mp")
        return (summed - target.astype(jnp.float32)).astype(jnp.bfloat16)

    resid = residual_of(weight.astype(jnp.bfloat16))
    ascent = jnp.dot(resid, everyone, preferred_element_type=jnp.float32)
    ascent_ms = lax.psum(jnp.sum(ascent * ascent), ("dp", "mp")) / entries
    perturbed = (weight + radius * jnp.tanh(ascent / jnp.sqrt(ascent_ms + epsilon))).astype(
        jnp.bfloat16
    )
    resid_two = residual_of(perturbed)
    descent = jnp.dot(resid_two, everyone, preferred_element_type=jnp.float32)
    descent_ms = lax.psum(jnp.sum(descent * descent), ("dp", "mp")) / entries
    return descent / jnp.sqrt(descent_ms + epsilon)


NEAR = (
    2.326819970068386e-2, -1.387039388740657e-1, 3.687424674597105e-1, -5.824733027278666e-1,
    6.210004621745983e-1, -4.944515323274145e-1, 3.404879937665872e-1, -2.741127028184656e-1,
    5.638259427386472e-1,
)
FAR = (
    -1.047766399936249e1, 1.297719955372516e1, -7.495518717768503e0, 2.921019019210786e0,
    -1.015265279202700e0, 4.218463358204948e-1, -2.820767439740514e-1, 5.641895067754075e-1,
)


def poly(coefficients, y):
    out = jnp.full_like(y, coefficients[0])
    for k in coefficients[1:]:
        out = out * y + k
    return out


def gelu(x):
    s = x * 0.7071067811865476
    t = jnp.maximum(-s, 1.0)
    q = 1.0 / t
    y = q * q
    tail = jnp.exp(-t * t) * q * jnp.where(t < 2.0, poly(NEAR, y), poly(FAR, y))
    return 0.5 * x * jnp.where(s > -1.0, 1.0 + lax.erf(s), tail)


def encode(x):
    return (x * jnp.abs(x)).astype(bf16)


def decode(y):
    y = y.astype(f32)
    return y * lax.rsqrt(jnp.maximum(jnp.abs(y), 1e-37))


def kernel(
    N, M, entries,
    pre_hbm, w_hbm, t_hbm, a, tot_ref,
    w, wl, h, x, tg, own, up_out, dn_out, up_in, dn_in, ssq, sm,
    ld, ags, agr, cs, cr, ss, sr,
):
    rows, ff = w.shape
    tokens = tg.shape[1]
    blk = tokens // N
    R = rows // TILE
    G = tokens // TILE
    C = R * G
    dp = lax.axis_index("dp")
    z = lax.axis_index("mp")
    b0 = lax.rem(dp, 2)
    b1 = lax.rem(dp // 2, 2)
    b2 = dp // 4
    ds_ = 1 - 2 * b0
    dx = 2 * (1 - 2 * b1)
    dy = 4 * (1 - 2 * b2)
    sib = dp + ds_
    p = dp + (1 - b0) * dx + b0 * dy
    q = dp + b0 * dx + (1 - b0) * dy
    diag = dp + dx + dy
    sibp = q + ds_
    sibq = p + ds_
    sibd = diag + ds_

    def load(i, src, dst):
        return pltpu.make_async_copy(src, dst, ld.at[i])

    def tok(b, lo=0, n=blk):
        return pl.ds(pl.multiple_of(b * blk + lo, 16), n)

    def rowg(r):
        return pl.ds(pl.multiple_of(r * TILE, TILE), TILE)

    load_x = load(0, pre_hbm, x)
    load_t = load(1, t_hbm, tg)
    load_w = [load(2 + r, w_hbm.at[rowg(r), :], w.at[rowg(r), :]) for r in range(R)]
    load_x.start()
    for lw in load_w:
        lw.start()
    load_t.start()

    barrier = pltpu.get_barrier_semaphore()
    dps = [lax.rem(dp + k, N) for k in range(N)]
    zs = [lax.rem(z + k, M) for k in range(M)]
    others = [(i, j) for i in range(N) for j in range(M) if i + j]
    for i, j in others:
        pl.semaphore_signal(barrier, inc=1, device_id=(dps[i], zs[j]), device_id_type=MESH)

    load_x.wait()

    def activate(i, _):
        rs = pl.ds(pl.multiple_of(i * 16, 16), 16)
        h[tok(dp, i * 16, 16), :] = gelu(x[rs, :].astype(f32)).astype(bf16)
        return 0

    lax.fori_loop(0, blk // 16, activate, 0)
    pl.semaphore_wait(barrier, N * M - 1)

    def gather(i, block, to):
        return pltpu.make_async_remote_copy(
            src_ref=h.at[tok(block), :], dst_ref=h.at[tok(block), :],
            send_sem=ags.at[i], recv_sem=agr.at[i],
            device_id=(to, z), device_id_type=MESH,
        )

    S, PP, SP, T, ST, RL, SR = range(7)
    sends = {
        S: gather(S, dp, sib), PP: gather(PP, dp, p), SP: gather(SP, p, sib), T: gather(T, sib, p),
        ST: gather(ST, sibq, sib), RL: gather(RL, sibp, p), SR: gather(SR, sibd, sib),
    }
    recvs = {
        S: gather(S, sib, sib), PP: gather(PP, p, p), SP: gather(SP, sibp, sib), T: gather(T, sibq, p),
        ST: gather(ST, q, sib), RL: gather(RL, sibd, p), SR: gather(SR, diag, sib),
    }
    sends[PP].start()
    sends[S].start()

    def cast(r):
        def run(i, _):
            rs = pl.ds(pl.multiple_of(r * TILE + i * 64, 64), 64)
            wl[rs, :] = w[rs, :].astype(bf16)
            return 0

        load_w[r].wait()
        lax.fori_loop(0, TILE // 64, run, 0)

    load_t.wait()

    @pl.when(z == 0)
    def _():
        up_in[...] = jnp.zeros_like(up_in)

    @pl.when(z == M - 1)
    def _():
        dn_in[...] = jnp.zeros_like(dn_in)

    order = [dp, sib, p, sibp, sibq, q, sibd, diag]

    def block_of(c):
        out = order[0] * 0
        for k in range(N):
            out = out + order[k] * (1 - jnp.minimum(jnp.abs(c - k), 1))
        return out

    UP, DOWN = range(2)
    zu = lax.rem(z + 1, M)
    zd = lax.rem(z + M - 1, M)

    def up(c):
        return pltpu.make_async_remote_copy(
            src_ref=up_out.at[c], dst_ref=up_in.at[c], send_sem=cs.at[UP, c], recv_sem=cr.at[UP, c],
            device_id=(dp, zu), device_id_type=MESH,
        )

    def down(c):
        return pltpu.make_async_remote_copy(
            src_ref=dn_out.at[c], dst_ref=dn_in.at[c], send_sem=cs.at[DOWN, c], recv_sem=cr.at[DOWN, c],
            device_id=(dp, zd), device_id_type=MESH,
        )

    K = up_out.shape[0] // C
    sub = TILE // K

    def store_own(t, d):
        for k in range(K):
            own[t * K + k] = d[k * sub:(k + 1) * sub]

    def chain(phase, produce, prepare, consume):
        hop = LAGS[phase]
        lag_up = hop * z
        lag_dn = hop * (M - 1 - z)
        lag = jnp.maximum(lag_up, lag_dn)

        def inside(c):
            return (c >= 0) & (c < C * K)

        def forward(s):
            cu = s - lag_up

            @pl.when((z > 0) & inside(cu))
            def _():
                up(cu).wait_recv()

                @pl.when(z < M - 1)
                def _():
                    up_out[cu] = encode(own[cu] + decode(up_in[cu]))
                    up(cu).start()

            cd = s - lag_dn

            @pl.when((z < M - 1) & inside(cd))
            def _():
                down(cd).wait_recv()

                @pl.when(z > 0)
                def _():
                    dn_out[cd] = encode(own[cd] + decode(dn_in[cd]))
                    down(cd).start()

        def make(s):
            @pl.when((s < C * K) & (lax.rem(s, K) == 0))
            def _():
                produce(s // K)

                @pl.when(z == 0)
                def _():
                    for k in range(K):
                        up_out[s + k] = encode(own[s + k])
                        up(s + k).start()

                @pl.when(z == M - 1)
                def _():
                    for k in range(K):
                        dn_out[s + k] = encode(own[s + k])
                        down(s + k).start()

                prepare(s // K)

        def step(s, _):
            forward(s)
            make(s)
            c = s - lag

            @pl.when(inside(c) & (lax.rem(c, K) == K - 1))
            def _():
                consume(c // K)

            return 0

        lax.fori_loop(0, C * K + hop * (M - 1), step, 0)

        def drain(c, _):
            @pl.when(z < M - 1)
            def _():
                up(c).wait_send()

            @pl.when(z > 0)
            def _():
                down(c).wait_send()

            return 0

        lax.fori_loop(0, C * K, drain, 0)

    def summed(t):
        return jnp.concatenate(
            [own[t * K + k] + decode(up_in[t * K + k]) + decode(dn_in[t * K + k]) for k in range(K)], axis=0
        )

    def squares(d):
        return (d * d).reshape(d.shape[0] // 8, 8, d.shape[1]).sum(axis=0)

    def gradient(resid, rs, g, right):
        d = jnp.dot(resid, right, preferred_element_type=f32)

        @pl.when(g == 0)
        def _():
            a[rs, :] = d

        @pl.when((g > 0) & (g < G - 1))
        def _():
            a[rs, :] += d

        @pl.when(g == G - 1)
        def _():
            total = a[rs, :] + d
            a[rs, :] = total
            ssq[...] += squares(total)

    def pair(g):
        return block_of(2 * g), block_of(2 * g + 1)

    def hidden_of(g):
        one, two = pair(g)
        return jnp.concatenate([h[tok(one), :], h[tok(two), :]], axis=0)

    def produce_one(s):
        g = s // R
        r = lax.rem(s, R)

        @pl.when(s == 0)
        def _():
            recvs[S].wait_recv()
            sends[T].start()

        @pl.when(s == R)
        def _():
            recvs[PP].wait_recv()
            sends[SP].start()
            recvs[SP].wait_recv()
            sends[RL].start()

        @pl.when(s == 2 * R)
        def _():
            recvs[T].wait_recv()
            sends[ST].start()
            recvs[ST].wait_recv()

        @pl.when(s == 3 * R)
        def _():
            recvs[RL].wait_recv()
            sends[SR].start()
            recvs[SR].wait_recv()

        store_own(s, lax.dot_general(
            wl[rowg(r), :], hidden_of(g), (((1,), (1,)), ((), ())), preferred_element_type=f32
        ))

    def prepare_one(s):
        for k in range(1, R):
            @pl.when(s == k - 1)
            def _():
                cast(k)

    def consume_one(c):
        g = c // R
        rs = rowg(lax.rem(c, R))
        one, two = pair(g)
        target = jnp.concatenate(
            [tg[rs, pl.ds(pl.multiple_of(b * blk, blk), blk)] for b in (one, two)], axis=1
        )
        resid = (summed(c) - target.astype(f32)).astype(bf16)
        gradient(resid, rs, g, hidden_of(g))

    ssq[...] = jnp.zeros_like(ssq)
    cast(0)
    chain(0, produce_one, prepare_one, consume_one)
    for i in range(7):
        sends[i].wait_send()

    def total_squares(rnd):
        v = ssq[...]
        part = v[:, 0:128]
        for k in range(1, v.shape[1] // 128):
            part = part + v[:, 128 * k:128 * (k + 1)]

        def small(i, j, src):
            return pltpu.make_async_remote_copy(
                src_ref=sm.at[rnd, src], dst_ref=sm.at[rnd, src],
                send_sem=ss.at[rnd, i * M + j], recv_sem=sr.at[rnd, i * M + j],
                device_id=(dps[i], zs[j]), device_id_type=MESH,
            )

        me = dp * M + z
        sm[rnd, me] = part.sum(axis=0, keepdims=True)
        for i, j in others:
            small(i, j, me).start()
        for i, j in others:
            small(i, j, dps[(N - i) % N] * M + zs[(M - j) % M]).wait_recv()
        got = sm[rnd].sum(axis=0)
        for i, j in others:
            small(i, j, me).wait_send()
        return jnp.sum(got, axis=1, keepdims=True)

    scale = 1.0 / jnp.sqrt(total_squares(0) / entries + epsilon)
    ssq[...] = jnp.zeros_like(ssq)

    def wide_cols(g):
        return pl.ds(pl.multiple_of(g * TILE, TILE), TILE)

    def perturb(start, count):
        def run(i, _):
            rs = pl.ds(pl.multiple_of(start + i * 16, 16), 16)
            wl[rs, :] = (w[rs, :] + radius * jnp.tanh(a[rs, :] * scale)).astype(bf16)
            return 0

        lax.fori_loop(0, count // 16, run, 0)

    def prepare_two(s):
        part = TILE // G

        @pl.when(s < C - G)
        def _():
            perturb(TILE + s * part, part)

    def produce_two(s):
        r = s // G
        g = lax.rem(s, G)

        store_own(s, lax.dot_general(
            wl[rowg(r), :], h[wide_cols(g), :], (((1,), (1,)), ((), ())), preferred_element_type=f32
        ))

    def consume_two(c):
        g = lax.rem(c, G)
        rs = rowg(c // G)
        resid = (summed(c) - tg[rs, wide_cols(g)].astype(f32)).astype(bf16)
        gradient(resid, rs, g, h[wide_cols(g), :])

    perturb(0, TILE)
    chain(1, produce_two, prepare_two, consume_two)
    tot_ref[...] = 1.0 / jnp.sqrt(total_squares(1) / entries + epsilon)


def finish(d_ref, s_ref, out_hbm, buf, sem):
    strips, n, _ = buf.shape

    def copy(i):
        return pltpu.make_async_copy(buf.at[i], out_hbm.at[pl.ds(i * n, n), :], sem.at[i])

    for i in range(strips):
        buf[i] = d_ref[i * n:(i + 1) * n, :] * s_ref[...]
        copy(i).start()
    for i in range(strips):
        copy(i).wait()


def on_device(N, M, pre, weight, target):
    rows, ff = weight.shape
    tokens = target.shape[1]
    entries = rows * ff * N * M
    C = (rows // TILE) * (tokens // TILE)
    sub = TILE // PIECES
    hbm = pl.BlockSpec(memory_space=pltpu.HBM)
    vmem = pl.BlockSpec(memory_space=pltpu.VMEM)
    descent, scale = pl.pallas_call(
        functools.partial(kernel, N, M, float(entries)),
        out_shape=(pltpu.VMEM((rows, ff), f32), pltpu.VMEM((1, 1), f32)),
        in_specs=[hbm, hbm, hbm],
        scratch_shapes=[
            pltpu.VMEM((rows, ff), f32),
            pltpu.VMEM((rows, ff), bf16),
            pltpu.VMEM((tokens, ff), bf16),
            pltpu.VMEM((tokens // N, ff), bf16),
            pltpu.VMEM((rows, tokens), bf16),
            pltpu.VMEM((C * PIECES, sub, TILE), f32),
            pltpu.VMEM((C * PIECES, sub, TILE), bf16),
            pltpu.VMEM((C * PIECES, sub, TILE), bf16),
            pltpu.VMEM((C * PIECES, sub, TILE), bf16),
            pltpu.VMEM((C * PIECES, sub, TILE), bf16),
            pltpu.VMEM((8, ff), f32),
            pltpu.VMEM((2, N * M, 1, 128), f32),
            pltpu.SemaphoreType.DMA((2 + rows // TILE,)),
            pltpu.SemaphoreType.DMA((7,)),
            pltpu.SemaphoreType.DMA((7,)),
            pltpu.SemaphoreType.DMA((2, C * PIECES)),
            pltpu.SemaphoreType.DMA((2, C * PIECES)),
            pltpu.SemaphoreType.DMA((2, N * M)),
            pltpu.SemaphoreType.DMA((2, N * M)),
        ],
        compiler_params=pltpu.CompilerParams(
            collective_id=0, has_side_effects=True, vmem_limit_bytes=50 << 20
        ),
    )(pre, weight, target)
    strips = 6
    return pl.pallas_call(
        finish,
        out_shape=jax.ShapeDtypeStruct((rows, ff), f32),
        in_specs=[vmem, vmem],
        out_specs=hbm,
        scratch_shapes=[
            pltpu.VMEM((strips, rows // strips, ff), f32),
            pltpu.SemaphoreType.DMA((strips,)),
        ],
        compiler_params=pltpu.CompilerParams(vmem_limit_bytes=24 << 20),
    )(descent, scale)


def solution(mesh):
    N, M = mesh.shape["dp"], mesh.shape["mp"]
    body = functools.partial(on_device, N, M) if (N, M) == (8, 4) else on_device_plain
    return jax.shard_map(
        body,
        mesh=mesh,
        in_specs=(P("dp", "mp"), P("dp", "mp"), P("dp", None)),
        out_specs=P("dp", "mp"),
        check_vma=False,
    )
```

```python
import functools

import jax
import jax.numpy as jnp
from jax import lax
from jax.experimental import pallas as pl
from jax.experimental.pallas import tpu as pltpu
from jax.sharding import PartitionSpec as P

radius = 0.005
epsilon = 1e-06
MESH = pl.DeviceIdType.MESH
f32, bf16 = jnp.float32, jnp.bfloat16
TILE = 256
PIECES = 2
LAGS = (3, 3)
AHEAD = 1
PARTS = 2
APART = 2


def on_device_plain(pre, weight, target):
    hidden = jax.nn.gelu(pre.astype(jnp.float32), approximate=False).astype(jnp.bfloat16)
    everyone = lax.all_gather(hidden, "dp", axis=0, tiled=True)
    entries = weight.shape[0] * weight.shape[1] * lax.axis_size("dp") * lax.axis_size("mp")

    def residual_of(matrix):
        partial_out = lax.dot_general(
            matrix, everyone, (((1,), (1,)), ((), ())), preferred_element_type=jnp.float32
        )
        summed = lax.psum(partial_out, "mp")
        return (summed - target.astype(jnp.float32)).astype(jnp.bfloat16)

    resid = residual_of(weight.astype(jnp.bfloat16))
    ascent = jnp.dot(resid, everyone, preferred_element_type=jnp.float32)
    ascent_ms = lax.psum(jnp.sum(ascent * ascent), ("dp", "mp")) / entries
    perturbed = (weight + radius * jnp.tanh(ascent / jnp.sqrt(ascent_ms + epsilon))).astype(
        jnp.bfloat16
    )
    resid_two = residual_of(perturbed)
    descent = jnp.dot(resid_two, everyone, preferred_element_type=jnp.float32)
    descent_ms = lax.psum(jnp.sum(descent * descent), ("dp", "mp")) / entries
    return descent / jnp.sqrt(descent_ms + epsilon)


NEAR = (
    2.326819970068386e-2, -1.387039388740657e-1, 3.687424674597105e-1, -5.824733027278666e-1,
    6.210004621745983e-1, -4.944515323274145e-1, 3.404879937665872e-1, -2.741127028184656e-1,
    5.638259427386472e-1,
)
FAR = (
    -1.047766399936249e1, 1.297719955372516e1, -7.495518717768503e0, 2.921019019210786e0,
    -1.015265279202700e0, 4.218463358204948e-1, -2.820767439740514e-1, 5.641895067754075e-1,
)


def poly(coefficients, y):
    out = jnp.full_like(y, coefficients[0])
    for k in coefficients[1:]:
        out = out * y + k
    return out


def gelu(x):
    s = x * 0.7071067811865476
    t = jnp.maximum(-s, 1.0)
    q = 1.0 / t
    y = q * q
    tail = jnp.exp(-t * t) * q * jnp.where(t < 2.0, poly(NEAR, y), poly(FAR, y))
    return 0.5 * x * jnp.where(s > -1.0, 1.0 + lax.erf(s), tail)


def encode(x):
    return (x * jnp.abs(x)).astype(bf16)


def decode(y):
    y = y.astype(f32)
    return y * lax.rsqrt(jnp.maximum(jnp.abs(y), 1e-37))


def kernel(
    N, M, entries,
    pre_hbm, w_hbm, t_hbm, a, tot_ref,
    w, wl, h, x, tg, own, up_out, dn_out, up_in, dn_in, ssq, sm,
    ld, ags, agr, cs, cr, ss, sr,
):
    rows, ff = w.shape
    tokens = tg.shape[1]
    blk = tokens // N
    R = rows // TILE
    G = tokens // TILE
    C = R * G
    dp = lax.axis_index("dp")
    z = lax.axis_index("mp")
    b0 = lax.rem(dp, 2)
    b1 = lax.rem(dp // 2, 2)
    b2 = dp // 4
    ds_ = 1 - 2 * b0
    dx = 2 * (1 - 2 * b1)
    dy = 4 * (1 - 2 * b2)
    sib = dp + ds_
    p = dp + (1 - b0) * dx + b0 * dy
    q = dp + b0 * dx + (1 - b0) * dy
    diag = dp + dx + dy
    sibp = q + ds_
    sibq = p + ds_
    sibd = diag + ds_

    def load(i, src, dst):
        return pltpu.make_async_copy(src, dst, ld.at[i])

    def tok(b, lo=0, n=blk):
        return pl.ds(pl.multiple_of(b * blk + lo, 16), n)

    def rowg(r):
        return pl.ds(pl.multiple_of(r * TILE, TILE), TILE)

    load_x = load(0, pre_hbm, x)
    load_t = load(1, t_hbm, tg)
    load_w = [load(2 + r, w_hbm.at[rowg(r), :], w.at[rowg(r), :]) for r in range(R)]
    load_x.start()
    for lw in load_w:
        lw.start()
    load_t.start()

    barrier = pltpu.get_barrier_semaphore()
    dps = [lax.rem(dp + k, N) for k in range(N)]
    zs = [lax.rem(z + k, M) for k in range(M)]
    others = [(i, j) for i in range(N) for j in range(M) if i + j]
    for i, j in others:
        pl.semaphore_signal(barrier, inc=1, device_id=(dps[i], zs[j]), device_id_type=MESH)

    load_x.wait()

    def activate(i, _):
        rs = pl.ds(pl.multiple_of(i * 16, 16), 16)
        h[tok(dp, i * 16, 16), :] = gelu(x[rs, :].astype(f32)).astype(bf16)
        return 0

    lax.fori_loop(0, blk // 16, activate, 0)
    pl.semaphore_wait(barrier, N * M - 1)

    cut = blk // PARTS

    class Sent:
        def __init__(self, i, block, to):
            self.parts = [
                pltpu.make_async_remote_copy(
                    src_ref=h.at[tok(block, k * cut, cut), :], dst_ref=h.at[tok(block, k * cut, cut), :],
                    send_sem=ags.at[i, k], recv_sem=agr.at[i, k],
                    device_id=(to, z), device_id_type=MESH,
                )
                for k in range(PARTS)
            ]

        def start(self):
            for part in self.parts:
                part.start()

        def wait_recv(self):
            for part in self.parts:
                part.wait_recv()

        def wait_send(self):
            for part in self.parts:
                part.wait_send()

    S, PP, SP, T, ST, RL, SR = range(7)
    sends = {
        S: Sent(S, dp, sib), PP: Sent(PP, dp, p), SP: Sent(SP, p, sib), T: Sent(T, sib, p),
        ST: Sent(ST, sibq, sib), RL: Sent(RL, sibp, p), SR: Sent(SR, sibd, sib),
    }
    recvs = {
        S: Sent(S, sib, sib), PP: Sent(PP, p, p), SP: Sent(SP, sibp, sib), T: Sent(T, sibq, p),
        ST: Sent(ST, q, sib), RL: Sent(RL, sibd, p), SR: Sent(SR, diag, sib),
    }
    sends[PP].start()
    sends[S].start()

    def cast(r):
        def run(i, _):
            rs = pl.ds(pl.multiple_of(r * TILE + i * 64, 64), 64)
            wl[rs, :] = w[rs, :].astype(bf16)
            return 0

        load_w[r].wait()
        lax.fori_loop(0, TILE // 64, run, 0)

    load_t.wait()

    @pl.when(z == 0)
    def _():
        up_in[...] = jnp.zeros_like(up_in)

    @pl.when(z == M - 1)
    def _():
        dn_in[...] = jnp.zeros_like(dn_in)

    order = [dp, sib, p, sibp, sibq, q, sibd, diag]

    def block_of(c):
        out = order[0] * 0
        for k in range(N):
            out = out + order[k] * (1 - jnp.minimum(jnp.abs(c - k), 1))
        return out

    UP, DOWN = range(2)
    zu = lax.rem(z + 1, M)
    zd = lax.rem(z + M - 1, M)

    def up(c):
        return pltpu.make_async_remote_copy(
            src_ref=up_out.at[c], dst_ref=up_in.at[c], send_sem=cs.at[UP, c], recv_sem=cr.at[UP, c],
            device_id=(dp, zu), device_id_type=MESH,
        )

    def down(c):
        return pltpu.make_async_remote_copy(
            src_ref=dn_out.at[c], dst_ref=dn_in.at[c], send_sem=cs.at[DOWN, c], recv_sem=cr.at[DOWN, c],
            device_id=(dp, zd), device_id_type=MESH,
        )

    K = up_out.shape[0] // C
    sub = TILE // K

    def store_own(t, d):
        for k in range(K):
            own[t * K + k] = d[k * sub:(k + 1) * sub]

    def chain(phase, relay, produce, prepare, consume):
        hop = LAGS[phase]
        lag_up = hop * z
        lag_dn = hop * (M - 1 - z)
        lag = jnp.maximum(lag_up, lag_dn)

        def inside(c):
            return (c >= 0) & (c < C * K)

        def forward(s):
            cu = s - lag_up

            @pl.when((z > 0) & inside(cu))
            def _():
                up(cu).wait_recv()

                @pl.when(z < M - 1)
                def _():
                    up_out[cu] = encode(own[cu] + decode(up_in[cu]))
                    up(cu).start()

            cd = s - lag_dn

            @pl.when((z < M - 1) & inside(cd))
            def _():
                down(cd).wait_recv()

                @pl.when(z > 0)
                def _():
                    dn_out[cd] = encode(own[cd] + decode(dn_in[cd]))
                    down(cd).start()

        def make(s):
            @pl.when((s < C * K) & (lax.rem(s, K) == 0))
            def _():
                produce(s // K)

                @pl.when(z == 0)
                def _():
                    for k in range(K):
                        up_out[s + k] = encode(own[s + k])
                        up(s + k).start()

                @pl.when(z == M - 1)
                def _():
                    for k in range(K):
                        dn_out[s + k] = encode(own[s + k])
                        down(s + k).start()

                prepare(s // K)

        def step(s, _):
            if relay is not None:
                relay(s)
            forward(s)
            make(s)
            c = s - lag

            @pl.when(inside(c) & (lax.rem(c, K) == K - 1))
            def _():
                consume(c // K)

            return 0

        lax.fori_loop(0, C * K + hop * (M - 1), step, 0)

    def drain():
        def run(c, _):
            @pl.when(z < M - 1)
            def _():
                up(c).wait_send()

            @pl.when(z > 0)
            def _():
                down(c).wait_send()

            return 0

        lax.fori_loop(0, C * K, run, 0)

    def summed(t):
        return jnp.concatenate(
            [own[t * K + k] + decode(up_in[t * K + k]) + decode(dn_in[t * K + k]) for k in range(K)], axis=0
        )

    def squares(d):
        return (d * d).reshape(d.shape[0] // 8, 8, d.shape[1]).sum(axis=0)

    def gradient(resid, rs, g, right):
        d = jnp.dot(resid, right, preferred_element_type=f32)

        @pl.when(g == 0)
        def _():
            a[rs, :] = d

        @pl.when((g > 0) & (g < G - 1))
        def _():
            a[rs, :] += d

        @pl.when(g == G - 1)
        def _():
            total = a[rs, :] + d
            a[rs, :] = total
            ssq[...] += squares(total)

    def pair(g):
        return block_of(2 * g), block_of(2 * g + 1)

    def hidden_of(g):
        one, two = pair(g)
        return jnp.concatenate([h[tok(one), :], h[tok(two), :]], axis=0)

    def relay_one(s):
        for g, (got, on) in enumerate(((PP, SP), (T, ST), (RL, SR)), 1):
            for k in range(PARTS):
                @pl.when(s == g * R * K - AHEAD - (PARTS - 1 - k) * APART)
                def _():
                    recvs[got].parts[k].wait_recv()
                    sends[on].parts[k].start()

    def produce_one(s):
        g = s // R
        r = lax.rem(s, R)

        @pl.when(s == 0)
        def _():
            recvs[S].wait_recv()
            sends[T].start()

        @pl.when(s == R)
        def _():
            recvs[SP].wait_recv()
            sends[RL].start()

        @pl.when(s == 2 * R)
        def _():
            recvs[ST].wait_recv()

        @pl.when(s == 3 * R)
        def _():
            recvs[SR].wait_recv()

        store_own(s, lax.dot_general(
            wl[rowg(r), :], hidden_of(g), (((1,), (1,)), ((), ())), preferred_element_type=f32
        ))

    def prepare_one(s):
        for k in range(1, R):
            @pl.when(s == k - 1)
            def _():
                cast(k)

    def consume_one(c):
        g = c // R
        rs = rowg(lax.rem(c, R))
        one, two = pair(g)
        target = jnp.concatenate(
            [tg[rs, pl.ds(pl.multiple_of(b * blk, blk), blk)] for b in (one, two)], axis=1
        )
        resid = (summed(c) - target.astype(f32)).astype(bf16)
        gradient(resid, rs, g, hidden_of(g))

    ssq[...] = jnp.zeros_like(ssq)
    cast(0)
    chain(0, relay_one, produce_one, prepare_one, consume_one)

    def total_squares(rnd, meanwhile):
        v = ssq[...]
        part = v[:, 0:128]
        for k in range(1, v.shape[1] // 128):
            part = part + v[:, 128 * k:128 * (k + 1)]

        def small(i, j, src):
            return pltpu.make_async_remote_copy(
                src_ref=sm.at[rnd, src], dst_ref=sm.at[rnd, src],
                send_sem=ss.at[rnd, i * M + j], recv_sem=sr.at[rnd, i * M + j],
                device_id=(dps[i], zs[j]), device_id_type=MESH,
            )

        me = dp * M + z
        sm[rnd, me] = part.sum(axis=0, keepdims=True)
        for i, j in others:
            small(i, j, me).start()
        meanwhile()
        for i, j in others:
            small(i, j, dps[(N - i) % N] * M + zs[(M - j) % M]).wait_recv()
        got = jnp.sum(sm[rnd].sum(axis=0), axis=1, keepdims=True)

        def leave():
            for i, j in others:
                small(i, j, me).wait_send()

        return 1.0 / jnp.sqrt(got / entries + epsilon), leave

    def meanwhile_one():
        drain()
        for i in range(7):
            sends[i].wait_send()
        ssq[...] = jnp.zeros_like(ssq)

    scale, leave_one = total_squares(0, meanwhile_one)

    def wide_cols(g):
        return pl.ds(pl.multiple_of(g * TILE, TILE), TILE)

    def perturb(start, count):
        def run(i, _):
            rs = pl.ds(pl.multiple_of(start + i * 16, 16), 16)
            wl[rs, :] = (w[rs, :] + radius * jnp.tanh(a[rs, :] * scale)).astype(bf16)
            return 0

        lax.fori_loop(0, count // 16, run, 0)

    def prepare_two(s):
        part = TILE // G

        @pl.when(s < C - G)
        def _():
            perturb(TILE + s * part, part)

    def produce_two(s):
        r = s // G
        g = lax.rem(s, G)

        store_own(s, lax.dot_general(
            wl[rowg(r), :], h[wide_cols(g), :], (((1,), (1,)), ((), ())), preferred_element_type=f32
        ))

    def consume_two(c):
        g = lax.rem(c, G)
        rs = rowg(c // G)
        resid = (summed(c) - tg[rs, wide_cols(g)].astype(f32)).astype(bf16)
        gradient(resid, rs, g, h[wide_cols(g), :])

    perturb(0, TILE)
    chain(1, None, produce_two, prepare_two, consume_two)
    def meanwhile_two():
        drain()
        leave_one()

    total, leave_two = total_squares(1, meanwhile_two)
    tot_ref[...] = total
    leave_two()


def finish(d_ref, s_ref, out_hbm, buf, sem):
    strips, n, _ = buf.shape

    def copy(i):
        return pltpu.make_async_copy(buf.at[i], out_hbm.at[pl.ds(i * n, n), :], sem.at[i])

    for i in range(strips):
        buf[i] = d_ref[i * n:(i + 1) * n, :] * s_ref[...]
        copy(i).start()
    for i in range(strips):
        copy(i).wait()


def on_device(N, M, pre, weight, target):
    rows, ff = weight.shape
    tokens = target.shape[1]
    entries = rows * ff * N * M
    C = (rows // TILE) * (tokens // TILE)
    sub = TILE // PIECES
    hbm = pl.BlockSpec(memory_space=pltpu.HBM)
    vmem = pl.BlockSpec(memory_space=pltpu.VMEM)
    descent, scale = pl.pallas_call(
        functools.partial(kernel, N, M, float(entries)),
        out_shape=(pltpu.VMEM((rows, ff), f32), pltpu.VMEM((1, 1), f32)),
        in_specs=[hbm, hbm, hbm],
        scratch_shapes=[
            pltpu.VMEM((rows, ff), f32),
            pltpu.VMEM((rows, ff), bf16),
            pltpu.VMEM((tokens, ff), bf16),
            pltpu.VMEM((tokens // N, ff), bf16),
            pltpu.VMEM((rows, tokens), bf16),
            pltpu.VMEM((C * PIECES, sub, TILE), f32),
            pltpu.VMEM((C * PIECES, sub, TILE), bf16),
            pltpu.VMEM((C * PIECES, sub, TILE), bf16),
            pltpu.VMEM((C * PIECES, sub, TILE), bf16),
            pltpu.VMEM((C * PIECES, sub, TILE), bf16),
            pltpu.VMEM((8, ff), f32),
            pltpu.VMEM((2, N * M, 1, 128), f32),
            pltpu.SemaphoreType.DMA((2 + rows // TILE,)),
            pltpu.SemaphoreType.DMA((7, PARTS)),
            pltpu.SemaphoreType.DMA((7, PARTS)),
            pltpu.SemaphoreType.DMA((2, C * PIECES)),
            pltpu.SemaphoreType.DMA((2, C * PIECES)),
            pltpu.SemaphoreType.DMA((2, N * M)),
            pltpu.SemaphoreType.DMA((2, N * M)),
        ],
        compiler_params=pltpu.CompilerParams(
            collective_id=0, has_side_effects=True, vmem_limit_bytes=50 << 20
        ),
    )(pre, weight, target)
    strips = 6
    return pl.pallas_call(
        finish,
        out_shape=jax.ShapeDtypeStruct((rows, ff), f32),
        in_specs=[vmem, vmem],
        out_specs=hbm,
        scratch_shapes=[
            pltpu.VMEM((strips, rows // strips, ff), f32),
            pltpu.SemaphoreType.DMA((strips,)),
        ],
        compiler_params=pltpu.CompilerParams(vmem_limit_bytes=24 << 20),
    )(descent, scale)


def solution(mesh):
    N, M = mesh.shape["dp"], mesh.shape["mp"]
    body = functools.partial(on_device, N, M) if (N, M) == (8, 4) else on_device_plain
    return jax.shard_map(
        body,
        mesh=mesh,
        in_specs=(P("dp", "mp"), P("dp", "mp"), P("dp", None)),
        out_specs=P("dp", "mp"),
        check_vma=False,
    )
```

```python
import functools

import jax
import jax.numpy as jnp
from jax import lax
from jax.experimental import pallas as pl
from jax.experimental.pallas import tpu as pltpu
from jax.sharding import PartitionSpec as P

radius = 0.005
epsilon = 1e-06
MESH = pl.DeviceIdType.MESH
f32, bf16 = jnp.float32, jnp.bfloat16
TILE = 256
PIECES = 2
LAGS = (3, 3)
AHEAD = 1
PARTS = 2
APART = 2


def on_device_plain(pre, weight, target):
    hidden = jax.nn.gelu(pre.astype(jnp.float32), approximate=False).astype(jnp.bfloat16)
    everyone = lax.all_gather(hidden, "dp", axis=0, tiled=True)
    entries = weight.shape[0] * weight.shape[1] * lax.axis_size("dp") * lax.axis_size("mp")

    def residual_of(matrix):
        partial_out = lax.dot_general(
            matrix, everyone, (((1,), (1,)), ((), ())), preferred_element_type=jnp.float32
        )
        summed = lax.psum(partial_out, "mp")
        return (summed - target.astype(jnp.float32)).astype(jnp.bfloat16)

    resid = residual_of(weight.astype(jnp.bfloat16))
    ascent = jnp.dot(resid, everyone, preferred_element_type=jnp.float32)
    ascent_ms = lax.psum(jnp.sum(ascent * ascent), ("dp", "mp")) / entries
    perturbed = (weight + radius * jnp.tanh(ascent / jnp.sqrt(ascent_ms + epsilon))).astype(
        jnp.bfloat16
    )
    resid_two = residual_of(perturbed)
    descent = jnp.dot(resid_two, everyone, preferred_element_type=jnp.float32)
    descent_ms = lax.psum(jnp.sum(descent * descent), ("dp", "mp")) / entries
    return descent / jnp.sqrt(descent_ms + epsilon)


NEAR = (
    2.326819970068386e-2, -1.387039388740657e-1, 3.687424674597105e-1, -5.824733027278666e-1,
    6.210004621745983e-1, -4.944515323274145e-1, 3.404879937665872e-1, -2.741127028184656e-1,
    5.638259427386472e-1,
)
FAR = (
    -1.047766399936249e1, 1.297719955372516e1, -7.495518717768503e0, 2.921019019210786e0,
    -1.015265279202700e0, 4.218463358204948e-1, -2.820767439740514e-1, 5.641895067754075e-1,
)


def poly(coefficients, y):
    out = jnp.full_like(y, coefficients[0])
    for k in coefficients[1:]:
        out = out * y + k
    return out


def gelu(x):
    s = x * 0.7071067811865476
    t = jnp.maximum(-s, 1.0)
    q = 1.0 / t
    y = q * q
    tail = jnp.exp(-t * t) * q * jnp.where(t < 2.0, poly(NEAR, y), poly(FAR, y))
    return 0.5 * x * jnp.where(s > -1.0, 1.0 + lax.erf(s), tail)


def encode(x):
    return (x * jnp.abs(x)).astype(bf16)


def decode(y):
    y = y.astype(f32)
    return y * lax.rsqrt(jnp.maximum(jnp.abs(y), 1e-37))


def kernel(
    N, M, entries,
    pre_hbm, w_hbm, t_hbm, a, tot_ref,
    w, wl, h, x, tg, own, up_out, dn_out, up_in, dn_in, ssq, sm,
    ld, ags, agr, cs, cr, ss, sr,
):
    rows, ff = w.shape
    tokens = tg.shape[1]
    blk = tokens // N
    R = rows // TILE
    G = tokens // TILE
    C = R * G
    dp = lax.axis_index("dp")
    z = lax.axis_index("mp")
    b0 = lax.rem(dp, 2)
    b1 = lax.rem(dp // 2, 2)
    b2 = dp // 4
    ds_ = 1 - 2 * b0
    dx = 2 * (1 - 2 * b1)
    dy = 4 * (1 - 2 * b2)
    sib = dp + ds_
    p = dp + (1 - b0) * dx + b0 * dy
    q = dp + b0 * dx + (1 - b0) * dy
    diag = dp + dx + dy
    sibp = q + ds_
    sibq = p + ds_
    sibd = diag + ds_

    def load(i, src, dst):
        return pltpu.make_async_copy(src, dst, ld.at[i])

    def tok(b, lo=0, n=blk):
        return pl.ds(pl.multiple_of(b * blk + lo, 16), n)

    def rowg(r):
        return pl.ds(pl.multiple_of(r * TILE, TILE), TILE)

    load_x = load(0, pre_hbm, x)
    load_t = load(1, t_hbm, tg)
    load_w = [load(2 + r, w_hbm.at[rowg(r), :], w.at[rowg(r), :]) for r in range(R)]
    load_x.start()
    for lw in load_w:
        lw.start()
    load_t.start()

    barrier = pltpu.get_barrier_semaphore()
    dps = [lax.rem(dp + k, N) for k in range(N)]
    zs = [lax.rem(z + k, M) for k in range(M)]
    others = [(i, j) for i in range(N) for j in range(M) if i + j]
    for i, j in others:
        pl.semaphore_signal(barrier, inc=1, device_id=(dps[i], zs[j]), device_id_type=MESH)

    load_x.wait()

    def activate(i, _):
        rs = pl.ds(pl.multiple_of(i * 16, 16), 16)
        h[tok(dp, i * 16, 16), :] = gelu(x[rs, :].astype(f32)).astype(bf16)
        return 0

    lax.fori_loop(0, blk // 16, activate, 0)
    pl.semaphore_wait(barrier, N * M - 1)

    cut = blk // PARTS

    class Sent:
        def __init__(self, i, block, to):
            self.parts = [
                pltpu.make_async_remote_copy(
                    src_ref=h.at[tok(block, k * cut, cut), :], dst_ref=h.at[tok(block, k * cut, cut), :],
                    send_sem=ags.at[i, k], recv_sem=agr.at[i, k],
                    device_id=(to, z), device_id_type=MESH,
                )
                for k in range(PARTS)
            ]

        def start(self):
            for part in self.parts:
                part.start()

        def wait_recv(self):
            for part in self.parts:
                part.wait_recv()

        def wait_send(self):
            for part in self.parts:
                part.wait_send()

    S, PP, SP, T, ST, RL, SR = range(7)
    sends = {
        S: Sent(S, dp, sib), PP: Sent(PP, dp, p), SP: Sent(SP, p, sib), T: Sent(T, sib, p),
        ST: Sent(ST, sibq, sib), RL: Sent(RL, sibp, p), SR: Sent(SR, sibd, sib),
    }
    recvs = {
        S: Sent(S, sib, sib), PP: Sent(PP, p, p), SP: Sent(SP, sibp, sib), T: Sent(T, sibq, p),
        ST: Sent(ST, q, sib), RL: Sent(RL, sibd, p), SR: Sent(SR, diag, sib),
    }
    sends[PP].start()
    sends[S].start()

    def cast(r):
        def run(i, _):
            rs = pl.ds(pl.multiple_of(r * TILE + i * 64, 64), 64)
            wl[rs, :] = w[rs, :].astype(bf16)
            return 0

        load_w[r].wait()
        lax.fori_loop(0, TILE // 64, run, 0)

    load_t.wait()

    @pl.when(z == 0)
    def _():
        up_in[...] = jnp.zeros_like(up_in)

    @pl.when(z == M - 1)
    def _():
        dn_in[...] = jnp.zeros_like(dn_in)

    order = [dp, sib, p, sibp, sibq, q, sibd, diag]

    def block_of(c):
        out = order[0] * 0
        for k in range(N):
            out = out + order[k] * (1 - jnp.minimum(jnp.abs(c - k), 1))
        return out

    UP, DOWN = range(2)
    zu = lax.rem(z + 1, M)
    zd = lax.rem(z + M - 1, M)

    def up(c):
        return pltpu.make_async_remote_copy(
            src_ref=up_out.at[c], dst_ref=up_in.at[c], send_sem=cs.at[UP, c], recv_sem=cr.at[UP, c],
            device_id=(dp, zu), device_id_type=MESH,
        )

    def down(c):
        return pltpu.make_async_remote_copy(
            src_ref=dn_out.at[c], dst_ref=dn_in.at[c], send_sem=cs.at[DOWN, c], recv_sem=cr.at[DOWN, c],
            device_id=(dp, zd), device_id_type=MESH,
        )

    K = up_out.shape[0] // C
    sub = TILE // K

    def store_own(t, d):
        for k in range(K):
            own[t * K + k] = d[k * sub:(k + 1) * sub]

    def chain(phase, relay, produce, prepare, consume):
        hop = LAGS[phase]
        lag_up = hop * z
        lag_dn = hop * (M - 1 - z)
        lag = jnp.maximum(lag_up, lag_dn)

        def inside(c):
            return (c >= 0) & (c < C * K)

        def forward(s):
            cu = s - lag_up

            @pl.when((z > 0) & inside(cu))
            def _():
                up(cu).wait_recv()

                @pl.when(z < M - 1)
                def _():
                    up_out[cu] = encode(own[cu] + decode(up_in[cu]))
                    up(cu).start()

            cd = s - lag_dn

            @pl.when((z < M - 1) & inside(cd))
            def _():
                down(cd).wait_recv()

                @pl.when(z > 0)
                def _():
                    dn_out[cd] = encode(own[cd] + decode(dn_in[cd]))
                    down(cd).start()

        def make(s):
            @pl.when((s < C * K) & (lax.rem(s, K) == 0))
            def _():
                produce(s // K)

                @pl.when(z == 0)
                def _():
                    for k in range(K):
                        up_out[s + k] = encode(own[s + k])
                        up(s + k).start()

                @pl.when(z == M - 1)
                def _():
                    for k in range(K):
                        dn_out[s + k] = encode(own[s + k])
                        down(s + k).start()

                prepare(s // K)

        def step(s, _):
            if relay is not None:
                relay(s)
            forward(s)
            make(s)
            c = s - lag

            @pl.when(inside(c) & (lax.rem(c, K) == K - 1))
            def _():
                consume(c // K)

            return 0

        lax.fori_loop(0, C * K + hop * (M - 1), step, 0)

    def drain():
        def run(c, _):
            @pl.when(z < M - 1)
            def _():
                up(c).wait_send()

            @pl.when(z > 0)
            def _():
                down(c).wait_send()

            return 0

        lax.fori_loop(0, C * K, run, 0)

    def summed(t):
        return jnp.concatenate(
            [own[t * K + k] + decode(up_in[t * K + k]) + decode(dn_in[t * K + k]) for k in range(K)], axis=0
        )

    def squares(d):
        return (d * d).reshape(d.shape[0] // 8, 8, d.shape[1]).sum(axis=0)

    def gradient(resid, rs, g, right):
        def product():
            return jnp.dot(resid, right(), preferred_element_type=f32)

        @pl.when(g == 0)
        def _():
            a[rs, :] = product()

        @pl.when((g > 0) & (g < G - 1))
        def _():
            a[rs, :] += product()

        @pl.when(g == G - 1)
        def _():
            total = a[rs, :] + product()
            a[rs, :] = total
            ssq[...] += squares(total)

    def pair(g):
        return block_of(2 * g), block_of(2 * g + 1)

    def hidden_of(g):
        one, two = pair(g)
        return jnp.concatenate([h[tok(one), :], h[tok(two), :]], axis=0)

    def relay_one(s):
        for g, (got, on) in enumerate(((PP, SP), (T, ST), (RL, SR)), 1):
            for k in range(PARTS):
                @pl.when(s == g * R * K - AHEAD - (PARTS - 1 - k) * APART)
                def _():
                    recvs[got].parts[k].wait_recv()
                    sends[on].parts[k].start()

    def produce_one(s):
        g = s // R
        r = lax.rem(s, R)

        @pl.when(s == 0)
        def _():
            recvs[S].wait_recv()
            sends[T].start()

        @pl.when(s == R)
        def _():
            recvs[SP].wait_recv()
            sends[RL].start()

        @pl.when(s == 2 * R)
        def _():
            recvs[ST].wait_recv()

        @pl.when(s == 3 * R)
        def _():
            recvs[SR].wait_recv()

        store_own(s, lax.dot_general(
            wl[rowg(r), :], hidden_of(g), (((1,), (1,)), ((), ())), preferred_element_type=f32
        ))

    def prepare_one(s):
        for k in range(1, R):
            @pl.when(s == k - 1)
            def _():
                cast(k)

    def consume_one(c):
        g = c // R
        rs = rowg(lax.rem(c, R))
        one, two = pair(g)
        target = jnp.concatenate(
            [tg[rs, pl.ds(pl.multiple_of(b * blk, blk), blk)] for b in (one, two)], axis=1
        )
        resid = (summed(c) - target.astype(f32)).astype(bf16)
        gradient(resid, rs, g, lambda: hidden_of(g))

    ssq[...] = jnp.zeros_like(ssq)
    cast(0)
    chain(0, relay_one, produce_one, prepare_one, consume_one)

    def total_squares(rnd, meanwhile):
        v = ssq[...]
        part = v[:, 0:128]
        for k in range(1, v.shape[1] // 128):
            part = part + v[:, 128 * k:128 * (k + 1)]

        def small(i, j, src):
            return pltpu.make_async_remote_copy(
                src_ref=sm.at[rnd, src], dst_ref=sm.at[rnd, src],
                send_sem=ss.at[rnd, i * M + j], recv_sem=sr.at[rnd, i * M + j],
                device_id=(dps[i], zs[j]), device_id_type=MESH,
            )

        me = dp * M + z
        sm[rnd, me] = part.sum(axis=0, keepdims=True)
        for i, j in others:
            small(i, j, me).start()
        meanwhile()
        for i, j in others:
            small(i, j, dps[(N - i) % N] * M + zs[(M - j) % M]).wait_recv()
        got = jnp.sum(sm[rnd].sum(axis=0), axis=1, keepdims=True)

        def leave():
            for i, j in others:
                small(i, j, me).wait_send()

        return 1.0 / jnp.sqrt(got / entries + epsilon), leave

    def meanwhile_one():
        drain()
        for i in range(7):
            sends[i].wait_send()
        ssq[...] = jnp.zeros_like(ssq)

    scale, leave_one = total_squares(0, meanwhile_one)

    def wide_cols(g):
        return pl.ds(pl.multiple_of(g * TILE, TILE), TILE)

    def perturb(start, count):
        def run(i, _):
            rs = pl.ds(pl.multiple_of(start + i * 32, 32), 32)
            wl[rs, :] = (w[rs, :] + radius * jnp.tanh(a[rs, :] * scale)).astype(bf16)
            return 0

        lax.fori_loop(0, count // 32, run, 0)

    def prepare_two(s):
        part = TILE // G

        @pl.when(s < C - G)
        def _():
            perturb(TILE + s * part, part)

    def produce_two(s):
        r = s // G
        g = lax.rem(s, G)

        store_own(s, lax.dot_general(
            wl[rowg(r), :], h[wide_cols(g), :], (((1,), (1,)), ((), ())), preferred_element_type=f32
        ))

    def consume_two(c):
        g = lax.rem(c, G)
        rs = rowg(c // G)
        resid = (summed(c) - tg[rs, wide_cols(g)].astype(f32)).astype(bf16)
        gradient(resid, rs, g, lambda: h[wide_cols(g), :])

    perturb(0, TILE)
    chain(1, None, produce_two, prepare_two, consume_two)
    def meanwhile_two():
        drain()
        leave_one()

    total, leave_two = total_squares(1, meanwhile_two)
    tot_ref[...] = total
    leave_two()


def finish(d_ref, s_ref, out_hbm, buf, sem):
    strips, n, _ = buf.shape

    def copy(i):
        return pltpu.make_async_copy(buf.at[i], out_hbm.at[pl.ds(i * n, n), :], sem.at[i])

    for i in range(strips):
        buf[i] = d_ref[i * n:(i + 1) * n, :] * s_ref[...]
        copy(i).start()
    for i in range(strips):
        copy(i).wait()


def on_device(N, M, pre, weight, target):
    rows, ff = weight.shape
    tokens = target.shape[1]
    entries = rows * ff * N * M
    C = (rows // TILE) * (tokens // TILE)
    sub = TILE // PIECES
    hbm = pl.BlockSpec(memory_space=pltpu.HBM)
    vmem = pl.BlockSpec(memory_space=pltpu.VMEM)
    descent, scale = pl.pallas_call(
        functools.partial(kernel, N, M, float(entries)),
        out_shape=(pltpu.VMEM((rows, ff), f32), pltpu.VMEM((1, 1), f32)),
        in_specs=[hbm, hbm, hbm],
        scratch_shapes=[
            pltpu.VMEM((rows, ff), f32),
            pltpu.VMEM((rows, ff), bf16),
            pltpu.VMEM((tokens, ff), bf16),
            pltpu.VMEM((tokens // N, ff), bf16),
            pltpu.VMEM((rows, tokens), bf16),
            pltpu.VMEM((C * PIECES, sub, TILE), f32),
            pltpu.VMEM((C * PIECES, sub, TILE), bf16),
            pltpu.VMEM((C * PIECES, sub, TILE), bf16),
            pltpu.VMEM((C * PIECES, sub, TILE), bf16),
            pltpu.VMEM((C * PIECES, sub, TILE), bf16),
            pltpu.VMEM((8, ff), f32),
            pltpu.VMEM((2, N * M, 1, 128), f32),
            pltpu.SemaphoreType.DMA((2 + rows // TILE,)),
            pltpu.SemaphoreType.DMA((7, PARTS)),
            pltpu.SemaphoreType.DMA((7, PARTS)),
            pltpu.SemaphoreType.DMA((2, C * PIECES)),
            pltpu.SemaphoreType.DMA((2, C * PIECES)),
            pltpu.SemaphoreType.DMA((2, N * M)),
            pltpu.SemaphoreType.DMA((2, N * M)),
        ],
        compiler_params=pltpu.CompilerParams(
            collective_id=0, has_side_effects=True, vmem_limit_bytes=50 << 20
        ),
    )(pre, weight, target)
    strips = 6
    return pl.pallas_call(
        finish,
        out_shape=jax.ShapeDtypeStruct((rows, ff), f32),
        in_specs=[vmem, vmem],
        out_specs=hbm,
        scratch_shapes=[
            pltpu.VMEM((strips, rows // strips, ff), f32),
            pltpu.SemaphoreType.DMA((strips,)),
        ],
        compiler_params=pltpu.CompilerParams(vmem_limit_bytes=24 << 20),
    )(descent, scale)


def solution(mesh):
    N, M = mesh.shape["dp"], mesh.shape["mp"]
    body = functools.partial(on_device, N, M) if (N, M) == (8, 4) else on_device_plain
    return jax.shard_map(
        body,
        mesh=mesh,
        in_specs=(P("dp", "mp"), P("dp", "mp"), P("dp", None)),
        out_specs=P("dp", "mp"),
        check_vma=False,
    )
```

```python
import functools

import jax
import jax.numpy as jnp
from jax import lax
from jax.experimental import pallas as pl
from jax.experimental.pallas import tpu as pltpu
from jax.sharding import PartitionSpec as P

radius = 0.005
epsilon = 1e-06
MESH = pl.DeviceIdType.MESH
f32, bf16 = jnp.float32, jnp.bfloat16
TILE = 256
PIECES = 2
LAGS = (3, 3)
AHEAD = 1
PARTS = 2
APART = 2


def on_device_plain(pre, weight, target):
    hidden = jax.nn.gelu(pre.astype(jnp.float32), approximate=False).astype(jnp.bfloat16)
    everyone = lax.all_gather(hidden, "dp", axis=0, tiled=True)
    entries = weight.shape[0] * weight.shape[1] * lax.axis_size("dp") * lax.axis_size("mp")

    def residual_of(matrix):
        partial_out = lax.dot_general(
            matrix, everyone, (((1,), (1,)), ((), ())), preferred_element_type=jnp.float32
        )
        summed = lax.psum(partial_out, "mp")
        return (summed - target.astype(jnp.float32)).astype(jnp.bfloat16)

    resid = residual_of(weight.astype(jnp.bfloat16))
    ascent = jnp.dot(resid, everyone, preferred_element_type=jnp.float32)
    ascent_ms = lax.psum(jnp.sum(ascent * ascent), ("dp", "mp")) / entries
    perturbed = (weight + radius * jnp.tanh(ascent / jnp.sqrt(ascent_ms + epsilon))).astype(
        jnp.bfloat16
    )
    resid_two = residual_of(perturbed)
    descent = jnp.dot(resid_two, everyone, preferred_element_type=jnp.float32)
    descent_ms = lax.psum(jnp.sum(descent * descent), ("dp", "mp")) / entries
    return descent / jnp.sqrt(descent_ms + epsilon)


NEAR = (
    2.326819970068386e-2, -1.387039388740657e-1, 3.687424674597105e-1, -5.824733027278666e-1,
    6.210004621745983e-1, -4.944515323274145e-1, 3.404879937665872e-1, -2.741127028184656e-1,
    5.638259427386472e-1,
)
FAR = (
    -1.047766399936249e1, 1.297719955372516e1, -7.495518717768503e0, 2.921019019210786e0,
    -1.015265279202700e0, 4.218463358204948e-1, -2.820767439740514e-1, 5.641895067754075e-1,
)


def poly(coefficients, y):
    out = jnp.full_like(y, coefficients[0])
    for k in coefficients[1:]:
        out = out * y + k
    return out


def gelu(x):
    s = x * 0.7071067811865476
    t = jnp.maximum(-s, 1.0)
    q = 1.0 / t
    y = q * q
    tail = jnp.exp(-t * t) * q * jnp.where(t < 2.0, poly(NEAR, y), poly(FAR, y))
    return 0.5 * x * jnp.where(s > -1.0, 1.0 + lax.erf(s), tail)


def encode(x):
    return (x * jnp.abs(x)).astype(bf16)


def decode(y):
    y = y.astype(f32)
    return y * lax.rsqrt(jnp.maximum(jnp.abs(y), 1e-37))


def kernel(
    N, M, entries,
    pre_hbm, w_hbm, t_hbm, a, tot_ref,
    w, wl, h, x, tg, own, up_out, dn_out, up_in, dn_in, ssq, sm,
    ld, ags, agr, cs, cr, ss, sr,
):
    rows, ff = w.shape
    tokens = tg.shape[1]
    blk = tokens // N
    R = rows // TILE
    G = tokens // TILE
    C = R * G
    dp = lax.axis_index("dp")
    z = lax.axis_index("mp")
    b0 = lax.rem(dp, 2)
    b1 = lax.rem(dp // 2, 2)
    b2 = dp // 4
    ds_ = 1 - 2 * b0
    dx = 2 * (1 - 2 * b1)
    dy = 4 * (1 - 2 * b2)
    sib = dp + ds_
    p = dp + (1 - b0) * dx + b0 * dy
    q = dp + b0 * dx + (1 - b0) * dy
    diag = dp + dx + dy
    sibp = q + ds_
    sibq = p + ds_
    sibd = diag + ds_

    def load(i, src, dst):
        return pltpu.make_async_copy(src, dst, ld.at[i])

    def tok(b, lo=0, n=blk):
        return pl.ds(pl.multiple_of(b * blk + lo, 16), n)

    def rowg(r):
        return pl.ds(pl.multiple_of(r * TILE, TILE), TILE)

    load_x = load(0, pre_hbm, x)
    load_t = load(1, t_hbm, tg)
    load_w = [load(2 + r, w_hbm.at[rowg(r), :], w.at[rowg(r), :]) for r in range(R)]
    load_x.start()
    for lw in load_w:
        lw.start()
    load_t.start()

    barrier = pltpu.get_barrier_semaphore()
    dps = [lax.rem(dp + k, N) for k in range(N)]
    zs = [lax.rem(z + k, M) for k in range(M)]
    others = [(i, j) for i in range(N) for j in range(M) if i + j]
    for i, j in others:
        pl.semaphore_signal(barrier, inc=1, device_id=(dps[i], zs[j]), device_id_type=MESH)

    load_x.wait()

    def activate(i, _):
        rs = pl.ds(pl.multiple_of(i * 16, 16), 16)
        h[tok(dp, i * 16, 16), :] = gelu(x[rs, :].astype(f32)).astype(bf16)
        return 0

    lax.fori_loop(0, blk // 16, activate, 0)
    pl.semaphore_wait(barrier, N * M - 1)

    cut = blk // PARTS

    class Sent:
        def __init__(self, i, block, to):
            self.parts = [
                pltpu.make_async_remote_copy(
                    src_ref=h.at[tok(block, k * cut, cut), :], dst_ref=h.at[tok(block, k * cut, cut), :],
                    send_sem=ags.at[i, k], recv_sem=agr.at[i, k],
                    device_id=(to, z), device_id_type=MESH,
                )
                for k in range(PARTS)
            ]

        def start(self):
            for part in self.parts:
                part.start()

        def wait_recv(self):
            for part in self.parts:
                part.wait_recv()

        def wait_send(self):
            for part in self.parts:
                part.wait_send()

    S, PP, SP, T, ST, RL, SR = range(7)
    sends = {
        S: Sent(S, dp, sib), PP: Sent(PP, dp, p), SP: Sent(SP, p, sib), T: Sent(T, sib, p),
        ST: Sent(ST, sibq, sib), RL: Sent(RL, sibp, p), SR: Sent(SR, sibd, sib),
    }
    recvs = {
        S: Sent(S, sib, sib), PP: Sent(PP, p, p), SP: Sent(SP, sibp, sib), T: Sent(T, sibq, p),
        ST: Sent(ST, q, sib), RL: Sent(RL, sibd, p), SR: Sent(SR, diag, sib),
    }
    sends[PP].start()
    sends[S].start()

    def cast(r):
        def run(i, _):
            rs = pl.ds(pl.multiple_of(r * TILE + i * 64, 64), 64)
            wl[rs, :] = w[rs, :].astype(bf16)
            return 0

        load_w[r].wait()
        lax.fori_loop(0, TILE // 64, run, 0)

    load_t.wait()

    @pl.when(z == 0)
    def _():
        up_in[...] = jnp.zeros_like(up_in)

    @pl.when(z == M - 1)
    def _():
        dn_in[...] = jnp.zeros_like(dn_in)

    order = [dp, sib, p, sibp, sibq, q, sibd, diag]

    def block_of(c):
        out = order[0] * 0
        for k in range(N):
            out = out + order[k] * (1 - jnp.minimum(jnp.abs(c - k), 1))
        return out

    UP, DOWN = range(2)
    zu = lax.rem(z + 1, M)
    zd = lax.rem(z + M - 1, M)

    def up(c):
        return pltpu.make_async_remote_copy(
            src_ref=up_out.at[c], dst_ref=up_in.at[c], send_sem=cs.at[UP, c], recv_sem=cr.at[UP, c],
            device_id=(dp, zu), device_id_type=MESH,
        )

    def down(c):
        return pltpu.make_async_remote_copy(
            src_ref=dn_out.at[c], dst_ref=dn_in.at[c], send_sem=cs.at[DOWN, c], recv_sem=cr.at[DOWN, c],
            device_id=(dp, zd), device_id_type=MESH,
        )

    K = up_out.shape[0] // C
    sub = TILE // K

    def store_own(t, d):
        for k in range(K):
            own[t * K + k] = d[k * sub:(k + 1) * sub]

    def chain(phase, relay, produce, prepare, consume):
        hop = LAGS[phase]
        lag_up = hop * z
        lag_dn = hop * (M - 1 - z)
        lag = jnp.maximum(lag_up, lag_dn)

        def inside(c):
            return (c >= 0) & (c < C * K)

        def forward(s):
            cu = s - lag_up

            @pl.when((z > 0) & inside(cu))
            def _():
                up(cu).wait_recv()

                @pl.when(z < M - 1)
                def _():
                    up_out[cu] = encode(own[cu] + decode(up_in[cu]))
                    up(cu).start()

            cd = s - lag_dn

            @pl.when((z < M - 1) & inside(cd))
            def _():
                down(cd).wait_recv()

                @pl.when(z > 0)
                def _():
                    dn_out[cd] = encode(own[cd] + decode(dn_in[cd]))
                    down(cd).start()

        def make(s):
            @pl.when((s < C * K) & (lax.rem(s, K) == 0))
            def _():
                produce(s // K)

                @pl.when(z == 0)
                def _():
                    for k in range(K):
                        up_out[s + k] = encode(own[s + k])
                        up(s + k).start()

                @pl.when(z == M - 1)
                def _():
                    for k in range(K):
                        dn_out[s + k] = encode(own[s + k])
                        down(s + k).start()

                prepare(s // K)

        def step(s, _):
            if relay is not None:
                relay(s)
            forward(s)
            c = s - lag

            @pl.when(inside(c) & (lax.rem(c, K) == K - 1))
            def _():
                consume(c // K)

            make(s)
            return 0

        lax.fori_loop(0, C * K + hop * (M - 1), step, 0)

    def drain():
        def run(c, _):
            @pl.when(z < M - 1)
            def _():
                up(c).wait_send()

            @pl.when(z > 0)
            def _():
                down(c).wait_send()

            return 0

        lax.fori_loop(0, C * K, run, 0)

    def summed(t):
        return jnp.concatenate(
            [own[t * K + k] + decode(up_in[t * K + k]) + decode(dn_in[t * K + k]) for k in range(K)], axis=0
        )

    def squares(d):
        return (d * d).reshape(d.shape[0] // 8, 8, d.shape[1]).sum(axis=0)

    def gradient(resid, rs, g, right):
        def product():
            return jnp.dot(resid, right(), preferred_element_type=f32)

        @pl.when(g == 0)
        def _():
            a[rs, :] = product()

        @pl.when((g > 0) & (g < G - 1))
        def _():
            a[rs, :] += product()

        @pl.when(g == G - 1)
        def _():
            total = a[rs, :] + product()
            a[rs, :] = total
            ssq[...] += squares(total)

    def pair(g):
        return block_of(2 * g), block_of(2 * g + 1)

    def hidden_of(g):
        one, two = pair(g)
        return jnp.concatenate([h[tok(one), :], h[tok(two), :]], axis=0)

    def relay_one(s):
        for g, (got, on) in enumerate(((PP, SP), (T, ST), (RL, SR)), 1):
            for k in range(PARTS):
                @pl.when(s == g * R * K - AHEAD - (PARTS - 1 - k) * APART)
                def _():
                    recvs[got].parts[k].wait_recv()
                    sends[on].parts[k].start()

    def produce_one(s):
        g = s // R
        r = lax.rem(s, R)

        @pl.when(s == 0)
        def _():
            recvs[S].wait_recv()
            sends[T].start()

        @pl.when(s == R)
        def _():
            recvs[SP].wait_recv()
            sends[RL].start()

        @pl.when(s == 2 * R)
        def _():
            recvs[ST].wait_recv()

        @pl.when(s == 3 * R)
        def _():
            recvs[SR].wait_recv()

        store_own(s, lax.dot_general(
            wl[rowg(r), :], hidden_of(g), (((1,), (1,)), ((), ())), preferred_element_type=f32
        ))

    def prepare_one(s):
        for k in range(1, R):
            @pl.when(s == k - 1)
            def _():
                cast(k)

    def consume_one(c):
        g = c // R
        rs = rowg(lax.rem(c, R))
        one, two = pair(g)
        target = jnp.concatenate(
            [tg[rs, pl.ds(pl.multiple_of(b * blk, blk), blk)] for b in (one, two)], axis=1
        )
        resid = (summed(c) - target.astype(f32)).astype(bf16)
        gradient(resid, rs, g, lambda: hidden_of(g))

    ssq[...] = jnp.zeros_like(ssq)
    cast(0)
    chain(0, relay_one, produce_one, prepare_one, consume_one)

    def total_squares(rnd, meanwhile):
        v = ssq[...]
        part = v[:, 0:128]
        for k in range(1, v.shape[1] // 128):
            part = part + v[:, 128 * k:128 * (k + 1)]

        def small(i, j, src):
            return pltpu.make_async_remote_copy(
                src_ref=sm.at[rnd, src], dst_ref=sm.at[rnd, src],
                send_sem=ss.at[rnd, i * M + j], recv_sem=sr.at[rnd, i * M + j],
                device_id=(dps[i], zs[j]), device_id_type=MESH,
            )

        me = dp * M + z
        sm[rnd, me] = part.sum(axis=0, keepdims=True)
        for i, j in others:
            small(i, j, me).start()
        meanwhile()
        for i, j in others:
            small(i, j, dps[(N - i) % N] * M + zs[(M - j) % M]).wait_recv()
        got = jnp.sum(sm[rnd].sum(axis=0), axis=1, keepdims=True)

        def leave():
            for i, j in others:
                small(i, j, me).wait_send()

        return 1.0 / jnp.sqrt(got / entries + epsilon), leave

    def meanwhile_one():
        drain()
        for i in range(7):
            sends[i].wait_send()
        ssq[...] = jnp.zeros_like(ssq)

    scale, leave_one = total_squares(0, meanwhile_one)

    def wide_cols(g):
        return pl.ds(pl.multiple_of(g * TILE, TILE), TILE)

    def perturb(start, count):
        def run(i, _):
            rs = pl.ds(pl.multiple_of(start + i * 32, 32), 32)
            wl[rs, :] = (w[rs, :] + radius * jnp.tanh(a[rs, :] * scale)).astype(bf16)
            return 0

        lax.fori_loop(0, count // 32, run, 0)

    def prepare_two(s):
        part = TILE // G

        @pl.when(s < C - G)
        def _():
            perturb(TILE + s * part, part)

    def produce_two(s):
        r = s // G
        g = lax.rem(s, G)

        store_own(s, lax.dot_general(
            wl[rowg(r), :], h[wide_cols(g), :], (((1,), (1,)), ((), ())), preferred_element_type=f32
        ))

    def consume_two(c):
        g = lax.rem(c, G)
        rs = rowg(c // G)
        resid = (summed(c) - tg[rs, wide_cols(g)].astype(f32)).astype(bf16)
        gradient(resid, rs, g, lambda: h[wide_cols(g), :])

    perturb(0, TILE)
    chain(1, None, produce_two, prepare_two, consume_two)
    def meanwhile_two():
        drain()
        leave_one()

    total, leave_two = total_squares(1, meanwhile_two)
    tot_ref[...] = total
    leave_two()


def finish(d_ref, s_ref, out_hbm, buf, sem):
    strips, n, _ = buf.shape

    def copy(i):
        return pltpu.make_async_copy(buf.at[i], out_hbm.at[pl.ds(i * n, n), :], sem.at[i])

    for i in range(strips):
        buf[i] = d_ref[i * n:(i + 1) * n, :] * s_ref[...]
        copy(i).start()
    for i in range(strips):
        copy(i).wait()


def on_device(N, M, pre, weight, target):
    rows, ff = weight.shape
    tokens = target.shape[1]
    entries = rows * ff * N * M
    C = (rows // TILE) * (tokens // TILE)
    sub = TILE // PIECES
    hbm = pl.BlockSpec(memory_space=pltpu.HBM)
    vmem = pl.BlockSpec(memory_space=pltpu.VMEM)
    descent, scale = pl.pallas_call(
        functools.partial(kernel, N, M, float(entries)),
        out_shape=(pltpu.VMEM((rows, ff), f32), pltpu.VMEM((1, 1), f32)),
        in_specs=[hbm, hbm, hbm],
        scratch_shapes=[
            pltpu.VMEM((rows, ff), f32),
            pltpu.VMEM((rows, ff), bf16),
            pltpu.VMEM((tokens, ff), bf16),
            pltpu.VMEM((tokens // N, ff), bf16),
            pltpu.VMEM((rows, tokens), bf16),
            pltpu.VMEM((C * PIECES, sub, TILE), f32),
            pltpu.VMEM((C * PIECES, sub, TILE), bf16),
            pltpu.VMEM((C * PIECES, sub, TILE), bf16),
            pltpu.VMEM((C * PIECES, sub, TILE), bf16),
            pltpu.VMEM((C * PIECES, sub, TILE), bf16),
            pltpu.VMEM((8, ff), f32),
            pltpu.VMEM((2, N * M, 1, 128), f32),
            pltpu.SemaphoreType.DMA((2 + rows // TILE,)),
            pltpu.SemaphoreType.DMA((7, PARTS)),
            pltpu.SemaphoreType.DMA((7, PARTS)),
            pltpu.SemaphoreType.DMA((2, C * PIECES)),
            pltpu.SemaphoreType.DMA((2, C * PIECES)),
            pltpu.SemaphoreType.DMA((2, N * M)),
            pltpu.SemaphoreType.DMA((2, N * M)),
        ],
        compiler_params=pltpu.CompilerParams(
            collective_id=0, has_side_effects=True, vmem_limit_bytes=50 << 20
        ),
    )(pre, weight, target)
    strips = 6
    return pl.pallas_call(
        finish,
        out_shape=jax.ShapeDtypeStruct((rows, ff), f32),
        in_specs=[vmem, vmem],
        out_specs=hbm,
        scratch_shapes=[
            pltpu.VMEM((strips, rows // strips, ff), f32),
            pltpu.SemaphoreType.DMA((strips,)),
        ],
        compiler_params=pltpu.CompilerParams(vmem_limit_bytes=24 << 20),
    )(descent, scale)


def solution(mesh):
    N, M = mesh.shape["dp"], mesh.shape["mp"]
    body = functools.partial(on_device, N, M) if (N, M) == (8, 4) else on_device_plain
    return jax.shard_map(
        body,
        mesh=mesh,
        in_specs=(P("dp", "mp"), P("dp", "mp"), P("dp", None)),
        out_specs=P("dp", "mp"),
        check_vma=False,
    )
```
